32 devices in a mesh: groups: 2 (over y), tiles: 4 (over z), section: 4 (over x, core).
Axes of the slice: x: 2, y: 2, z: 4, core: 2. Of those that a mesh axis runs over, the one named last changes fastest.
Arguments:
- latents: float32 [4, 192, 8, 128], P('groups', None, 'tiles'), parts along dimension 0, may hold values from -6 to 6
- conv_weight: float32 [4, 27, 192, 192], P('section'), may hold values from -0.078125 to 0.078125
- gain: float32 [4, 192], P('section'), may hold values from 0.1 to 1.9
Outputs:
- decoded: float32 [4, 192, 8, 128], P('groups', 'section', 'tiles'), parts along dimension 0
The draws below stay inside these ranges and needn't reach their ends.
There are 2 independent parts, one for each index of `groups`. The reference program is written for one: setup_inputs(seed, part) draws one part's arguments, and reference() takes and returns one part's arrays. A program takes and returns all parts, laid end to end along the dimension named above; an argument that names none is the same for every part. Nothing has to cross between parts.
All inputs are finite; a program needn't handle non-finite values.
Results may differ from the reference program's by a relative error of at most 0.00013.
Values sent between devices are 32-bit elements; how exact they have to be, the bound alone decides.
No kernel may reach another device: no remote copies, remote signals or barrier semaphores. Data moves between devices by JAX's collectives and lax.ppermute only.
A program may use at most 64 MiB of HBM per device.

```python
import jax
import jax.numpy as jnp
from jax import lax

C = 192
W = 128
FRAMES = 2
LAYERS = 4
HEIGHT = 8


def block_scale(stream_key, extent, cuts, low, high):
    level = 1.0
    for position, parts in cuts:
        steps = jax.random.uniform(jax.random.fold_in(jax.random.fold_in(stream_key, 6), position), (parts,), jnp.float32, low / len(cuts), high / len(cuts))
        level = level * jnp.repeat(jnp.exp(steps), extent[position] // parts).reshape((-1,) + (1,) * (len(extent) - 1 - position))
    return level


def scatter_about(own_key, dims, deviation, limit, shards=(), kind=jnp.bfloat16):
    values = jax.random.normal(own_key, dims, jnp.float32) * deviation
    if len(shards) > 0:
        values = block_scale(own_key, dims, shards, -0.22, 0.18) * values
    return jnp.clip(values, min=-limit, max=limit).astype(kind)


def setup_inputs(seed: int = 0, part: int = 0) -> dict:
    key_of = jax.random.split(jax.random.key(seed), 4)
    part_splits = jax.random.split(jax.random.fold_in(key_of[3], part), 4)
    latents = scatter_about(part_splits[0], (FRAMES, C, HEIGHT, W), 1.0, 6.0, ((2, 4),), jnp.float32)
    conv_weight = scatter_about(key_of[1], (LAYERS, 27, C, C), (27 * C) ** -0.5, 0.078125, ((0, 4),), jnp.float32)
    gain = jnp.clip(1.0 + 0.18 * jax.random.normal(key_of[2], (LAYERS, C), jnp.float32), 0.1, 1.9)
    return dict(latents=latents, conv_weight=conv_weight, gain=gain)


def normalize(values, gain_row):
    meansq = lax.optimization_barrier(jnp.mean(values * values, axis=1, keepdims=True))
    scaled = values * lax.rsqrt(meansq + 1e-06) * gain_row[None, :, None, None]
    return jax.nn.silu(scaled)

def reference(latents, conv_weight, gain):
    current = latents
    for layer in range(LAYERS):
        normed = normalize(current, gain[layer])
        kernel = conv_weight[layer].reshape(3, 3, 3, C, C).transpose(3, 4, 0, 1, 2)
        inputs = normed.transpose(1, 0, 2, 3)[None]
        result = lax.conv_general_dilated(inputs, kernel, (1, 1, 1), ((2, 0), (1, 1), (1, 1)), dimension_numbers=('NCDHW', 'OIDHW', 'NCDHW'), precision=lax.Precision.HIGHEST)
        current = current + result[0].transpose(1, 0, 2, 3)
    return current
```

```python
import jax
import jax.numpy as jnp
from jax import lax
from jax.experimental import pallas as pl
from jax.experimental.pallas import tpu as pltpu
from jax.sharding import PartitionSpec as P

EPSILON = 1e-06
VMEM = pl.BlockSpec(memory_space=pltpu.VMEM)
ANY = pl.BlockSpec(memory_space=pl.ANY)


def partner_a(tile, tiles):
    other = tile ^ 1
    return other if other < tiles else tile


def partner_b(tile, tiles):
    other = ((tile - 1) ^ 1) + 1 if tile > 0 else tile
    return other if other < tiles else tile


def idle_cycle(where, names):
    for k, name in enumerate(names):
        where[name] = names[(k + 1) % len(names)]


def section_hop(layer, sections):
    where = {}
    if layer % 2 == 0:
        idle_cycle(where, [layer, layer + 1])
    elif layer + 2 < sections:
        idle_cycle(where, [layer - 1, layer, layer + 1, layer + 2])
    else:
        idle_cycle(where, [layer - 1, layer, layer + 1])
    taken = set(where)
    for s in range(sections):
        if s not in taken:
            where[s] = s ^ 1 if (s ^ 1) not in taken and (s ^ 1) < sections else s
    return where


def hop_pairs(layer, tiles, sections, tile_of):
    hop = section_hop(layer, sections)
    pairs = []
    for t in range(tiles):
        for s in range(sections):
            goal = tile_of(t) if s == layer else t
            pairs.append((t * sections + s, goal * sections + hop[s]))
    return pairs


def rim_pairs(tiles, sections, tile_of):
    pairs = []
    for t in range(tiles):
        where = {}
        if tile_of(t) == t:
            for s in range(sections):
                where[s] = s ^ 1 if (s ^ 1) < sections else s
        else:
            idle_cycle(where, list(range(1, sections)))
        for s in range(sections):
            if s == 0 and tile_of(t) != t:
                pairs.append((t * sections, tile_of(t) * sections))
            else:
                pairs.append((t * sections + s, t * sections + where[s]))
    return pairs


def share_pairs(target, tiles, sections):
    last = sections - 1
    where = {}
    if target == last - 1 or (target ^ 1) >= last - 1:
        idle_cycle(where, [last, target])
    else:
        idle_cycle(where, [last, target, target ^ 1, last - 1])
    taken = set(where)
    for s in range(sections):
        if s not in taken:
            where[s] = s ^ 1 if (s ^ 1) not in taken and (s ^ 1) < sections else s
    return [
        (t * sections + s, t * sections + where[s])
        for t in range(tiles)
        for s in range(sections)
    ]


def send(value, pairs):
    return lax.ppermute(value, ("tiles", "section"), pairs)


def split(values):
    high = values.astype(jnp.bfloat16)
    low = (values - high.astype(jnp.float32)).astype(jnp.bfloat16)
    return high, low


def prepare_kernel(first, depth, weight, high, low, staged, sems):
    count, channels = staged.shape[0], staged.shape[1]
    copies = []
    for k in range(count):
        copies.append(
            pltpu.make_async_copy(weight.at[first + k], staged.at[k], sems.at[k])
        )
        copies[-1].start()
    for a in range(count // 9):
        for k in range(0, 9, 2):
            copies[9 * a + k].wait()
            parts = [staged[9 * a + k]]
            if k + 1 < 9:
                copies[9 * a + k + 1].wait()
                parts.append(staged[9 * a + k + 1])
                width = 2 * channels
            else:
                width = depth - 8 * channels
                if width > channels:
                    parts.append(jnp.zeros((channels, width - channels), jnp.float32))
            block = jnp.concatenate(parts, axis=1)
            upper, lower = split(block)
            high[a, :, k * channels : k * channels + width] = upper
            low[a, :, k * channels : k * channels + width] = lower


def prepare(weight, steps, depth):
    channels = weight.shape[1]
    shape = jax.ShapeDtypeStruct((steps, channels, depth), jnp.bfloat16)

    def kernel(*refs):
        prepare_kernel(9 * (3 - steps), depth, *refs)

    return pl.pallas_call(
        kernel,
        out_shape=(shape, shape),
        in_specs=[ANY],
        out_specs=(VMEM, VMEM),
        scratch_shapes=[
            pltpu.VMEM((9 * steps, channels, channels), jnp.float32),
            pltpu.SemaphoreType.DMA((9 * steps,)),
        ],
        name="prepare",
    )(weight)


def normalize(values, gain):
    meansq = jnp.mean(values * values, axis=0, keepdims=True)
    scaled = values * lax.rsqrt(meansq + EPSILON) * gain
    return scaled / (1.0 + jnp.exp(-scaled))


def shifted(values, col_off):
    if col_off == 1:
        return values
    width = values.shape[1]
    lane = lax.broadcasted_iota(jnp.int32, values.shape, 1)
    if col_off == 0:
        return jnp.where(lane == 0, 0.0, pltpu.roll(values, 1, 1))
    return jnp.where(lane == width - 1, 0.0, pltpu.roll(values, width - 1, 1))


def product(high, low, patch_high, patch_low):
    def dot(a, b):
        return jnp.dot(a, b, preferred_element_type=jnp.float32)

    return dot(high, patch_high) + dot(low, patch_high) + dot(high, patch_low)


def frame_step(layer, tiles, main, near_a, near_b, gain, weights, partial, keep):
    channels, width = near_a.shape
    rows = main.shape[0] // channels
    steps, _, depth = weights[0].shape
    block = jax.ShapeDtypeStruct(main.shape, jnp.float32)
    edge = jax.ShapeDtypeStruct(near_a.shape, jnp.float32)
    patch = jax.ShapeDtypeStruct((depth, rows * width), jnp.bfloat16)

    def kernel(*refs):
        main_ref, a_ref, b_ref, gain_ref, high_ref, low_ref = refs[:6]
        refs = refs[6:]
        if partial is not None:
            partial_ref, refs = refs[0], refs[1:]
        out_ref, out_a_ref, out_b_ref, patch_high, patch_low = refs
        tile = lax.axis_index("tiles")
        even = lax.rem(tile, 2) == 0

        @pl.when(lax.axis_index("section") == layer)
        def _():
            gains = gain_ref[...]
            near_one, near_two = a_ref[...], b_ref[...]
            above = jnp.where(even, near_two, near_one)
            below = jnp.where(even, near_one, near_two)
            above = jnp.where(tile == 0, 0.0, above)
            below = jnp.where(tile == tiles - 1, 0.0, below)
            own = [main_ref[r * channels : (r + 1) * channels, :] for r in range(rows)]
            if depth > 9 * channels:
                pad = jnp.zeros((depth - 9 * channels, rows * width), jnp.bfloat16)
                patch_high[9 * channels :, :] = pad
                patch_low[9 * channels :, :] = pad
            for q, source in enumerate([above] + own + [below]):
                normed = normalize(source, gains)
                for e in range(3):
                    upper, lower = split(shifted(normed, e))
                    for b in range(3):
                        r = q - b
                        if 0 <= r < rows:
                            k = (3 * b + e) * channels
                            cols = slice(r * width, (r + 1) * width)
                            patch_high[k : k + channels, cols] = upper
                            patch_low[k : k + channels, cols] = lower
            total = product(
                high_ref[steps - 1], low_ref[steps - 1], patch_high[...], patch_low[...]
            )
            if partial is not None:
                total = total + partial_ref[...]
            results = [
                own[r] + total[:, r * width : (r + 1) * width] for r in range(rows)
            ]
            for r in range(rows):
                out_ref[r * channels : (r + 1) * channels, :] = results[r]
            out_a_ref[...] = jnp.where(even, results[-1], results[0])
            out_b_ref[...] = jnp.where(even, results[0], results[-1])

    operands = [main, near_a, near_b, gain, *weights]
    if partial is not None:
        operands.append(partial)
    flops = 6 * channels * depth * rows * width
    out_shape = [block, edge, edge]
    scratch = []
    if keep:
        out_shape += [patch, patch]
    else:
        scratch = [pltpu.VMEM(patch.shape, patch.dtype)] * 2
    return pl.pallas_call(
        kernel,
        out_shape=tuple(out_shape),
        in_specs=[VMEM] * len(operands),
        out_specs=tuple([VMEM] * len(out_shape)),
        scratch_shapes=scratch,
        cost_estimate=pl.CostEstimate(
            flops=flops, bytes_accessed=2**20, transcendentals=0
        ),
        name="frame_step",
    )(*operands)


def earlier_frames(layer, weights, patches):
    steps, channels, depth = weights[0].shape
    count = len(patches)
    columns = patches[0][0].shape[1]

    def kernel(high_ref, low_ref, *refs):
        out_ref = refs[-1]

        @pl.when(lax.axis_index("section") == layer)
        def _():
            total = None
            for n in range(count):
                a = steps - 1 - (count - n)
                term = product(
                    high_ref[a], low_ref[a], refs[2 * n][...], refs[2 * n + 1][...]
                )
                total = term if total is None else total + term
            out_ref[...] = total

    operands = [*weights]
    for pair in patches:
        operands += list(pair)
    return pl.pallas_call(
        kernel,
        out_shape=jax.ShapeDtypeStruct((channels, columns), jnp.float32),
        in_specs=[VMEM] * len(operands),
        out_specs=VMEM,
        cost_estimate=pl.CostEstimate(
            flops=6 * channels * depth * columns * count,
            bytes_accessed=2**20,
            transcendentals=0,
        ),
        name="earlier_frames",
    )(*operands)


def local(latents, conv_weight, gain):
    frames, channels, rows, width = latents.shape
    tiles, sections = lax.axis_size("tiles"), lax.axis_size("section")
    tile, section = lax.axis_index("tiles"), lax.axis_index("section")
    depth = -(-9 * channels // 256) * 256
    steps = min(frames, 3)
    of_a = lambda t: partner_a(t, tiles)
    of_b = lambda t: partner_b(t, tiles)

    even = lax.rem(tile, 2) == 0
    by_row = jnp.transpose(latents, (0, 2, 1, 3))
    main = [by_row[f].reshape(rows * channels, width) for f in range(frames)]
    edge_a = [jnp.where(even, by_row[f, -1], by_row[f, 0]) for f in range(frames)]
    edge_b = [jnp.where(even, by_row[f, 0], by_row[f, -1]) for f in range(frames)]
    rim_a, rim_b = (rim_pairs(tiles, sections, of) for of in (of_a, of_b))
    near_a = [send(edge_a[f], rim_a) for f in range(frames)]
    near_b = [send(edge_b[f], rim_b) for f in range(frames)]
    weights = prepare(conv_weight[0], steps, depth)
    gains = gain.reshape(channels, 1)

    for layer in range(sections):
        if layer > 0:
            straight = hop_pairs(layer - 1, tiles, sections, lambda t: t)
            cross_a = hop_pairs(layer - 1, tiles, sections, of_a)
            cross_b = hop_pairs(layer - 1, tiles, sections, of_b)
            main = [send(value, straight) for value in main]
            near_a = [send(value, cross_a) for value in edge_a]
            near_b = [send(value, cross_b) for value in edge_b]
        patches, next_main, edge_a, edge_b = [], [], [], []
        for f in range(frames):
            partial = None
            if f > 0:
                partial = earlier_frames(layer, weights, patches[-2:])
            keep = f < frames - 1
            done = frame_step(
                layer, tiles, main[f], near_a[f], near_b[f], gains, weights, partial, keep
            )
            next_main.append(done[0])
            edge_a.append(done[1])
            edge_b.append(done[2])
            if keep:
                patches.append(done[3:])
        main = next_main

    share = channels // sections
    outs = []
    for f in range(frames):
        cube = main[f].reshape(rows, channels, width)
        own = cube[:, (sections - 1) * share :]
        for target in range(sections - 1):
            part = cube[:, target * share : (target + 1) * share]
            got = send(
                part.reshape(rows * share, width), share_pairs(target, tiles, sections)
            )
            own = jnp.where(section == target, got.reshape(rows, share, width), own)
        outs.append(own)
    return jnp.transpose(jnp.stack(outs), (0, 2, 1, 3))


def solution(mesh):
    return jax.shard_map(
        local,
        mesh=mesh,
        in_specs=(
            P("groups", None, "tiles", None),
            P("section", None, None, None),
            P("section", None),
        ),
        out_specs=P("groups", "section", "tiles", None),
        check_vma=False,
    )
```

```python
import jax
import jax.numpy as jnp
from jax import lax
from jax.experimental import pallas as pl
from jax.experimental.pallas import tpu as pltpu
from jax.sharding import PartitionSpec as P

EPSILON = 1e-06
GRANT = pltpu.CompilerParams(vmem_limit_bytes=12 * 2**20)
VMEM = pl.BlockSpec(memory_space=pltpu.VMEM)
ANY = pl.BlockSpec(memory_space=pl.ANY)


def partner_a(tile, tiles):
    other = tile ^ 1
    return other if other < tiles else tile


def partner_b(tile, tiles):
    other = ((tile - 1) ^ 1) + 1 if tile > 0 else tile
    return other if other < tiles else tile


def idle_cycle(where, names):
    for k, name in enumerate(names):
        where[name] = names[(k + 1) % len(names)]


def section_hop(layer, sections):
    where = {}
    if layer % 2 == 0:
        idle_cycle(where, [layer, layer + 1])
    elif layer + 2 < sections:
        idle_cycle(where, [layer - 1, layer, layer + 1, layer + 2])
    else:
        idle_cycle(where, [layer - 1, layer, layer + 1])
    taken = set(where)
    for s in range(sections):
        if s not in taken:
            where[s] = s ^ 1 if (s ^ 1) not in taken and (s ^ 1) < sections else s
    return where


def hop_pairs(layer, tiles, sections, tile_of):
    hop = section_hop(layer, sections)
    pairs = []
    for t in range(tiles):
        for s in range(sections):
            goal = tile_of(t) if s == layer else t
            pairs.append((t * sections + s, goal * sections + hop[s]))
    return pairs


def rim_pairs(tiles, sections, tile_of):
    pairs = []
    for t in range(tiles):
        where = {}
        if tile_of(t) == t:
            for s in range(sections):
                where[s] = s ^ 1 if (s ^ 1) < sections else s
        else:
            idle_cycle(where, list(range(1, sections)))
        for s in range(sections):
            if s == 0 and tile_of(t) != t:
                pairs.append((t * sections, tile_of(t) * sections))
            else:
                pairs.append((t * sections + s, t * sections + where[s]))
    return pairs


def share_pairs(target, tiles, sections):
    last = sections - 1
    where = {}
    if target == last - 1 or (target ^ 1) >= last - 1:
        idle_cycle(where, [last, target])
    else:
        idle_cycle(where, [last, target, target ^ 1, last - 1])
    taken = set(where)
    for s in range(sections):
        if s not in taken:
            where[s] = s ^ 1 if (s ^ 1) not in taken and (s ^ 1) < sections else s
    return [
        (t * sections + s, t * sections + where[s])
        for t in range(tiles)
        for s in range(sections)
    ]


def send(value, pairs):
    return lax.ppermute(value, ("tiles", "section"), pairs)


def split(values):
    high = values.astype(jnp.bfloat16)
    low = (values - high.astype(jnp.float32)).astype(jnp.bfloat16)
    return high, low


def prepare_kernel(first, depth, weight, high, low, staged, sems):
    count, channels = staged.shape[0], staged.shape[1]
    copies = []
    for k in range(count):
        copies.append(
            pltpu.make_async_copy(weight.at[first + k], staged.at[k], sems.at[k])
        )
        copies[-1].start()
    for a in range(count // 9):
        for k in range(0, 9, 2):
            copies[9 * a + k].wait()
            parts = [staged[9 * a + k]]
            if k + 1 < 9:
                copies[9 * a + k + 1].wait()
                parts.append(staged[9 * a + k + 1])
                width = 2 * channels
            else:
                width = depth - 8 * channels
                if width > channels:
                    parts.append(jnp.zeros((channels, width - channels), jnp.float32))
            block = jnp.concatenate(parts, axis=1)
            upper, lower = split(block)
            high[a, :, k * channels : k * channels + width] = upper
            low[a, :, k * channels : k * channels + width] = lower


def prepare(weight, steps, depth):
    channels = weight.shape[1]
    shape = jax.ShapeDtypeStruct((steps, channels, depth), jnp.bfloat16)

    def kernel(*refs):
        prepare_kernel(9 * (3 - steps), depth, *refs)

    return pl.pallas_call(
        kernel,
        out_shape=(shape, shape),
        in_specs=[ANY],
        out_specs=(VMEM, VMEM),
        scratch_shapes=[
            pltpu.VMEM((9 * steps, channels, channels), jnp.float32),
            pltpu.SemaphoreType.DMA((9 * steps,)),
        ],
        compiler_params=GRANT,
        name="prepare",
    )(weight)


def normalize(values, gain):
    meansq = jnp.mean(values * values, axis=0, keepdims=True)
    scaled = values * lax.rsqrt(meansq + EPSILON) * gain
    return scaled / (1.0 + jnp.exp(-scaled))


def shifted(values, col_off):
    if col_off == 1:
        return values
    width = values.shape[1]
    lane = lax.broadcasted_iota(jnp.int32, values.shape, 1)
    if col_off == 0:
        return jnp.where(lane == 0, 0.0, pltpu.roll(values, 1, 1))
    return jnp.where(lane == width - 1, 0.0, pltpu.roll(values, width - 1, 1))


def product(high, low, patch_high, patch_low):
    def dot(a, b):
        return jnp.dot(a, b, preferred_element_type=jnp.float32)

    return dot(high, patch_high) + dot(low, patch_high) + dot(high, patch_low)


def frame_step(layer, tiles, main, near_a, near_b, gain, weights, partial, keep):
    channels, width = near_a.shape
    rows = main.shape[0] // channels
    steps, _, depth = weights[0].shape
    block = jax.ShapeDtypeStruct(main.shape, jnp.float32)
    edge = jax.ShapeDtypeStruct(near_a.shape, jnp.float32)
    patch = jax.ShapeDtypeStruct((depth, rows * width), jnp.bfloat16)

    def kernel(*refs):
        main_ref, a_ref, b_ref, gain_ref, high_ref, low_ref = refs[:6]
        refs = refs[6:]
        if partial is not None:
            partial_ref, refs = refs[0], refs[1:]
        out_ref, out_a_ref, out_b_ref, patch_high, patch_low = refs
        tile = lax.axis_index("tiles")
        even = lax.rem(tile, 2) == 0

        @pl.when(lax.axis_index("section") == layer)
        def _():
            gains = gain_ref[...]
            near_one, near_two = a_ref[...], b_ref[...]
            above = jnp.where(even, near_two, near_one)
            below = jnp.where(even, near_one, near_two)
            above = jnp.where(tile == 0, 0.0, above)
            below = jnp.where(tile == tiles - 1, 0.0, below)
            own = [main_ref[r * channels : (r + 1) * channels, :] for r in range(rows)]
            if depth > 9 * channels:
                pad = jnp.zeros((depth - 9 * channels, rows * width), jnp.bfloat16)
                patch_high[9 * channels :, :] = pad
                patch_low[9 * channels :, :] = pad
            for q, source in enumerate([above] + own + [below]):
                normed = normalize(source, gains)
                for e in range(3):
                    upper, lower = split(shifted(normed, e))
                    for b in range(3):
                        r = q - b
                        if 0 <= r < rows:
                            k = (3 * b + e) * channels
                            cols = slice(r * width, (r + 1) * width)
                            patch_high[k : k + channels, cols] = upper
                            patch_low[k : k + channels, cols] = lower
            total = product(
                high_ref[steps - 1], low_ref[steps - 1], patch_high[...], patch_low[...]
            )
            if partial is not None:
                total = total + partial_ref[...]
            results = [
                own[r] + total[:, r * width : (r + 1) * width] for r in range(rows)
            ]
            for r in range(rows):
                out_ref[r * channels : (r + 1) * channels, :] = results[r]
            out_a_ref[...] = jnp.where(even, results[-1], results[0])
            out_b_ref[...] = jnp.where(even, results[0], results[-1])

    operands = [main, near_a, near_b, gain, *weights]
    if partial is not None:
        operands.append(partial)
    flops = 6 * channels * depth * rows * width
    out_shape = [block, edge, edge]
    scratch = []
    if keep:
        out_shape += [patch, patch]
    else:
        scratch = [pltpu.VMEM(patch.shape, patch.dtype)] * 2
    return pl.pallas_call(
        kernel,
        out_shape=tuple(out_shape),
        in_specs=[VMEM] * len(operands),
        out_specs=tuple([VMEM] * len(out_shape)),
        scratch_shapes=scratch,
        cost_estimate=pl.CostEstimate(
            flops=flops, bytes_accessed=2**20, transcendentals=0
        ),
        compiler_params=GRANT,
        name="frame_step",
    )(*operands)


def earlier_frames(layer, weights, patches):
    steps, channels, depth = weights[0].shape
    count = len(patches)
    columns = patches[0][0].shape[1]

    def kernel(high_ref, low_ref, *refs):
        out_ref = refs[-1]

        @pl.when(lax.axis_index("section") == layer)
        def _():
            total = None
            for n in range(count):
                a = steps - 1 - (count - n)
                term = product(
                    high_ref[a], low_ref[a], refs[2 * n][...], refs[2 * n + 1][...]
                )
                total = term if total is None else total + term
            out_ref[...] = total

    operands = [*weights]
    for pair in patches:
        operands += list(pair)
    return pl.pallas_call(
        kernel,
        out_shape=jax.ShapeDtypeStruct((channels, columns), jnp.float32),
        in_specs=[VMEM] * len(operands),
        out_specs=VMEM,
        cost_estimate=pl.CostEstimate(
            flops=6 * channels * depth * columns * count,
            bytes_accessed=2**20,
            transcendentals=0,
        ),
        compiler_params=GRANT,
        name="earlier_frames",
    )(*operands)


def local(latents, conv_weight, gain):
    frames, channels, rows, width = latents.shape
    tiles, sections = lax.axis_size("tiles"), lax.axis_size("section")
    tile, section = lax.axis_index("tiles"), lax.axis_index("section")
    depth = -(-9 * channels // 256) * 256
    steps = min(frames, 3)
    of_a = lambda t: partner_a(t, tiles)
    of_b = lambda t: partner_b(t, tiles)

    even = lax.rem(tile, 2) == 0
    by_row = jnp.transpose(latents, (0, 2, 1, 3))
    main = [by_row[f].reshape(rows * channels, width) for f in range(frames)]
    edge_a = [jnp.where(even, by_row[f, -1], by_row[f, 0]) for f in range(frames)]
    edge_b = [jnp.where(even, by_row[f, 0], by_row[f, -1]) for f in range(frames)]
    rim_a, rim_b = (rim_pairs(tiles, sections, of) for of in (of_a, of_b))
    near_a = [send(edge_a[f], rim_a) for f in range(frames)]
    near_b = [send(edge_b[f], rim_b) for f in range(frames)]
    weights = prepare(conv_weight[0], steps, depth)
    gains = gain.reshape(channels, 1)

    for layer in range(sections):
        if layer > 0:
            straight = hop_pairs(layer - 1, tiles, sections, lambda t: t)
            cross_a = hop_pairs(layer - 1, tiles, sections, of_a)
            cross_b = hop_pairs(layer - 1, tiles, sections, of_b)
            main = [send(value, straight) for value in main]
            near_a = [send(value, cross_a) for value in edge_a]
            near_b = [send(value, cross_b) for value in edge_b]
        patches, next_main, edge_a, edge_b = [], [], [], []
        for f in range(frames):
            partial = None
            if f > 0:
                partial = earlier_frames(layer, weights, patches[-2:])
            keep = f < frames - 1
            done = frame_step(
                layer, tiles, main[f], near_a[f], near_b[f], gains, weights, partial, keep
            )
            next_main.append(done[0])
            edge_a.append(done[1])
            edge_b.append(done[2])
            if keep:
                patches.append(done[3:])
        main = next_main

    share = channels // sections
    outs = []
    for f in range(frames):
        cube = main[f].reshape(rows, channels, width)
        own = cube[:, (sections - 1) * share :]
        for target in range(sections - 1):
            part = cube[:, target * share : (target + 1) * share]
            got = send(
                part.reshape(rows * share, width), share_pairs(target, tiles, sections)
            )
            own = jnp.where(section == target, got.reshape(rows, share, width), own)
        outs.append(own)
    return jnp.transpose(jnp.stack(outs), (0, 2, 1, 3))


def solution(mesh):
    return jax.shard_map(
        local,
        mesh=mesh,
        in_specs=(
            P("groups", None, "tiles", None),
            P("section", None, None, None),
            P("section", None),
        ),
        out_specs=P("groups", "section", "tiles", None),
        check_vma=False,
    )
```

```python
import jax
import jax.numpy as jnp
from jax import lax
from jax.experimental import pallas as pl
from jax.experimental.pallas import tpu as pltpu
from jax.sharding import PartitionSpec as P


EPSILON = 1e-06
GRANT = pltpu.CompilerParams(vmem_limit_bytes=12 * 2**20)
VMEM = pl.BlockSpec(memory_space=pltpu.VMEM)
ANY = pl.BlockSpec(memory_space=pl.ANY)


def partner_a(tile, tiles):
    other = tile ^ 1
    return other if other < tiles else tile


def partner_b(tile, tiles):
    other = ((tile - 1) ^ 1) + 1 if tile > 0 else tile
    return other if other < tiles else tile


def idle_cycle(where, names):
    for k, name in enumerate(names):
        where[name] = names[(k + 1) % len(names)]


def section_hop(layer, sections):
    where = {}
    if layer % 2 == 0:
        idle_cycle(where, [layer, layer + 1])
    elif layer + 2 < sections:
        idle_cycle(where, [layer - 1, layer, layer + 1, layer + 2])
    else:
        idle_cycle(where, [layer - 1, layer, layer + 1])
    taken = set(where)
    for s in range(sections):
        if s not in taken:
            where[s] = s ^ 1 if (s ^ 1) not in taken and (s ^ 1) < sections else s
    return where


def hop_pairs(layer, tiles, sections, tile_of):
    hop = section_hop(layer, sections)
    pairs = []
    for t in range(tiles):
        for s in range(sections):
            goal = tile_of(t) if s == layer else t
            pairs.append((t * sections + s, goal * sections + hop[s]))
    return pairs


def rim_pairs(tiles, sections, tile_of):
    pairs = []
    for t in range(tiles):
        where = {}
        if tile_of(t) == t:
            for s in range(sections):
                where[s] = s ^ 1 if (s ^ 1) < sections else s
        else:
            idle_cycle(where, list(range(1, sections)))
        for s in range(sections):
            if s == 0 and tile_of(t) != t:
                pairs.append((t * sections, tile_of(t) * sections))
            else:
                pairs.append((t * sections + s, t * sections + where[s]))
    return pairs


def share_pairs(target, tiles, sections):
    last = sections - 1
    where = {}
    if target == last - 1 or (target ^ 1) >= last - 1:
        idle_cycle(where, [last, target])
    else:
        idle_cycle(where, [last, target, target ^ 1, last - 1])
    taken = set(where)
    for s in range(sections):
        if s not in taken:
            where[s] = s ^ 1 if (s ^ 1) not in taken and (s ^ 1) < sections else s
    return [
        (t * sections + s, t * sections + where[s])
        for t in range(tiles)
        for s in range(sections)
    ]


def send(value, pairs):
    return lax.ppermute(value, ("tiles", "section"), pairs)


def split(values):
    high = values.astype(jnp.bfloat16)
    low = (values - high.astype(jnp.float32)).astype(jnp.bfloat16)
    return high, low


def held(shape, dtype=jnp.float32):
    return pltpu.VMEM(shape, dtype)


def prepare(weight, gain, steps, depth, width):
    channels = weight.shape[1]
    first = 9 * (3 - steps)
    groups = [(k, min(2, 9 - k)) for k in range(0, 9, 2)]

    def kernel(weight_ref, gain_ref, high, low, gains, staged, sems):
        copies = {}
        for a in reversed(range(steps)):
            for n, (k, size) in enumerate(groups):
                at = 9 * a + k
                copies[a, k] = pltpu.make_async_copy(
                    weight_ref.at[pl.ds(first + at, size)],
                    staged.at[pl.ds(at, size)],
                    sems.at[a, n],
                )
                copies[a, k].start()
        square = (channels, channels)
        lane = lax.broadcasted_iota(jnp.int32, square, 1)
        sublane = lax.broadcasted_iota(jnp.int32, square, 0)
        spread = jnp.broadcast_to(gain_ref[...], square)
        column = jnp.sum(jnp.where(lane == sublane, spread, 0.0), axis=1, keepdims=True)
        gains[...] = jnp.broadcast_to(column, (channels, width))
        for a in reversed(range(steps)):
            for k, size in groups:
                copies[a, k].wait()
                parts = [staged[9 * a + k + n] for n in range(size)]
                span = size * channels
                if k + size == 9 and depth > 9 * channels:
                    extra = depth - 9 * channels
                    parts.append(jnp.zeros((channels, extra), jnp.float32))
                    span += extra
                upper, lower = split(jnp.concatenate(parts, axis=1))
                high[a, :, k * channels : k * channels + span] = upper
                low[a, :, k * channels : k * channels + span] = lower

    shape = (steps, channels, depth)
    return pl.pallas_call(
        kernel,
        out_shape=(
            held(shape, jnp.bfloat16),
            held(shape, jnp.bfloat16),
            held((channels, width)),
        ),
        in_specs=[pl.BlockSpec(memory_space=pltpu.HBM), VMEM],
        out_specs=(VMEM, VMEM, VMEM),
        scratch_shapes=[
            pltpu.VMEM((9 * steps, channels, channels), jnp.float32),
            pltpu.SemaphoreType.DMA((steps, len(groups))),
        ],
        compiler_params=GRANT,
        name="prepare",
    )(pltpu.with_memory_space_constraint(weight, pltpu.HBM), gain)


def edges(latents, rows):
    frames, lines, width = latents.shape
    channels = lines // rows

    def kernel(ref, *outs):
        even = lax.rem(lax.axis_index("tiles"), 2) == 0
        for f in range(frames):
            top = ref[f, pl.ds(0, channels, stride=rows), :]
            bottom = ref[f, pl.ds(rows - 1, channels, stride=rows), :]
            outs[2 * f][...] = jnp.where(even, bottom, top)
            outs[2 * f + 1][...] = jnp.where(even, top, bottom)

    return pl.pallas_call(
        kernel,
        out_shape=tuple([held((channels, width))] * (2 * frames)),
        in_specs=[VMEM],
        out_specs=tuple([VMEM] * (2 * frames)),
        compiler_params=GRANT,
        name="edges",
    )(latents)


def normalize(values, gain):
    meansq = jnp.mean(values * values, axis=0, keepdims=True)
    scaled = values * lax.rsqrt(meansq + EPSILON) * gain
    return scaled / (1.0 + jnp.exp(-scaled))


def shifted(values, col_off):
    if col_off == 1:
        return values
    width = values.shape[1]
    lane = lax.broadcasted_iota(jnp.int32, values.shape, 1)
    if col_off == 0:
        return jnp.where(lane == 0, 0.0, pltpu.roll(values, 1, 1))
    return jnp.where(lane == width - 1, 0.0, pltpu.roll(values, width - 1, 1))


def product(high, low, patch_high, patch_low):
    def dot(a, b):
        return jnp.dot(a, b, preferred_element_type=jnp.float32)

    return dot(high, patch_high) + dot(low, patch_high) + dot(high, patch_low)


def frame_step(layer, tiles, sections, main, frame, near_a, near_b, gain, weights, partial, keep):
    channels, width = near_a.shape
    lines = main.shape[-2]
    rows = lines // channels
    steps, _, depth = weights[0].shape
    last = layer == sections - 1
    share = lines // sections
    count = sections if last else 3

    def kernel(*refs):
        main_ref, a_ref, b_ref, gain_ref, high_ref, low_ref = refs[:6]
        refs = refs[6:]
        if partial is not None:
            partial_ref, refs = refs[0], refs[1:]
        outs, (patch_high, patch_low) = refs[:count], refs[count:]
        tile = lax.axis_index("tiles")
        even = lax.rem(tile, 2) == 0

        @pl.when(lax.axis_index("section") == layer)
        def _():
            gains = gain_ref[...]
            near_one, near_two = a_ref[...], b_ref[...]
            above = jnp.where(even, near_two, near_one)
            below = jnp.where(even, near_one, near_two)
            above = jnp.where(tile == 0, 0.0, above)
            below = jnp.where(tile == tiles - 1, 0.0, below)
            own = []
            for r in range(rows):
                line = pl.ds(r, channels, stride=rows)
                own.append(main_ref[line, :] if frame is None else main_ref[frame, line, :])
            if depth > 9 * channels:
                pad = jnp.zeros((depth - 9 * channels, rows * width), jnp.bfloat16)
                patch_high[9 * channels :, :] = pad
                patch_low[9 * channels :, :] = pad
            for q, source in enumerate([above] + own + [below]):
                normed = normalize(source, gains)
                for e in range(3):
                    upper, lower = split(shifted(normed, e))
                    for b in range(3):
                        r = q - b
                        if 0 <= r < rows:
                            k = (3 * b + e) * channels
                            cols = slice(r * width, (r + 1) * width)
                            patch_high[k : k + channels, cols] = upper
                            patch_low[k : k + channels, cols] = lower
            total = product(
                high_ref[steps - 1], low_ref[steps - 1], patch_high[...], patch_low[...]
            )
            if partial is not None:
                total = total + partial_ref[...]
            results = [
                own[r] + total[:, r * width : (r + 1) * width] for r in range(rows)
            ]
            if last:
                part = share // rows
                for s in range(sections):
                    for r in range(rows):
                        outs[s][pl.ds(r, part, stride=rows), :] = results[r][
                            s * part : (s + 1) * part
                        ]
            else:
                for r in range(rows):
                    outs[0][pl.ds(r, channels, stride=rows), :] = results[r]
                outs[1][...] = jnp.where(even, results[-1], results[0])
                outs[2][...] = jnp.where(even, results[0], results[-1])

    operands = [main, near_a, near_b, gain, *weights]
    if partial is not None:
        operands.append(partial)
    if last:
        out_shape = [held((share, width))] * sections
    else:
        out_shape = [held((lines, width)), held(near_a.shape), held(near_a.shape)]
    patch = held((depth, rows * width), jnp.bfloat16)
    scratch = []
    if keep:
        out_shape += [patch, patch]
    else:
        scratch = [patch, patch]
    return pl.pallas_call(
        kernel,
        out_shape=tuple(out_shape),
        in_specs=[VMEM] * len(operands),
        out_specs=tuple([VMEM] * len(out_shape)),
        scratch_shapes=scratch,
        cost_estimate=pl.CostEstimate(
            flops=6 * channels * depth * rows * width,
            bytes_accessed=2**20,
            transcendentals=0,
        ),
        compiler_params=GRANT,
        name="frame_step",
    )(*operands)


def earlier_frames(layer, weights, patches):
    steps, channels, depth = weights[0].shape
    count = len(patches)
    columns = patches[0][0].shape[1]

    def kernel(high_ref, low_ref, *refs):
        out_ref = refs[-1]

        @pl.when(lax.axis_index("section") == layer)
        def _():
            total = None
            for n in range(count):
                a = steps - 1 - (count - n)
                term = product(
                    high_ref[a], low_ref[a], refs[2 * n][...], refs[2 * n + 1][...]
                )
                total = term if total is None else total + term
            out_ref[...] = total

    operands = [*weights]
    for pair in patches:
        operands += list(pair)
    return pl.pallas_call(
        kernel,
        out_shape=held((channels, columns)),
        in_specs=[VMEM] * len(operands),
        out_specs=VMEM,
        cost_estimate=pl.CostEstimate(
            flops=6 * channels * depth * columns * count,
            bytes_accessed=2**20,
            transcendentals=0,
        ),
        compiler_params=GRANT,
        name="earlier_frames",
    )(*operands)


def local(latents, conv_weight, gain):
    frames, channels, rows, width = latents.shape
    tiles, sections = lax.axis_size("tiles"), lax.axis_size("section")
    section = lax.axis_index("section")
    depth = -(-9 * channels // 256) * 256
    steps = min(frames, 3)
    of_a = lambda t: partner_a(t, tiles)
    of_b = lambda t: partner_b(t, tiles)

    flat = latents.reshape(frames, channels * rows, width)
    edge = edges(flat, rows)
    edge_a, edge_b = edge[0::2], edge[1::2]
    rim_a, rim_b = (rim_pairs(tiles, sections, of) for of in (of_a, of_b))
    near_a, near_b = [], []
    for f in range(frames):
        near_a.append(send(edge_a[f], rim_a))
        near_b.append(send(edge_b[f], rim_b))
    *weights, gains = prepare(conv_weight[0], gain, steps, depth, width)
    main = [flat] * frames

    for layer in range(sections):
        if layer > 0:
            straight = hop_pairs(layer - 1, tiles, sections, lambda t: t)
            cross_a = hop_pairs(layer - 1, tiles, sections, of_a)
            cross_b = hop_pairs(layer - 1, tiles, sections, of_b)
            main = [send(main[f], straight) for f in range(frames)]
            near_a = [send(edge_a[f], cross_a) for f in range(frames)]
            near_b = [send(edge_b[f], cross_b) for f in range(frames)]
        patches, next_main, edge_a, edge_b = [], [], [], []
        for f in range(frames):
            partial = None
            if f > 0:
                partial = earlier_frames(layer, weights, patches[-2:])
            keep = f < frames - 1
            done = frame_step(
                layer, tiles, sections, main[f], f if layer == 0 else None,
                near_a[f], near_b[f], gains, weights, partial, keep,
            )
            if keep:
                patches.append(done[-2:])
                done = done[:-2]
            next_main.append(done if layer == sections - 1 else done[0])
            edge_a.append(done[1])
            edge_b.append(done[2])
        main = next_main

    outs = []
    for f in range(frames):
        own = main[f][sections - 1]
        for target in range(sections - 1):
            pairs = share_pairs(target, tiles, sections)
            got = send(main[f][target], pairs)
            own = jnp.where(section == target, got, own)
        outs.append(own)
    return jnp.stack(outs).reshape(frames, channels // sections, rows, width)


def solution(mesh):
    return jax.shard_map(
        local,
        mesh=mesh,
        in_specs=(
            P("groups", None, "tiles", None),
            P("section", None, None, None),
            P("section", None),
        ),
        out_specs=P("groups", "section", "tiles", None),
        check_vma=False,
    )
```

```python
import jax
import jax.numpy as jnp
from jax import lax
from jax.experimental import pallas as pl
from jax.experimental.pallas import tpu as pltpu
from jax.sharding import PartitionSpec as P


EPSILON = 1e-06
GRANT = pltpu.CompilerParams(vmem_limit_bytes=12 * 2**20)
VMEM = pl.BlockSpec(memory_space=pltpu.VMEM)
HBM = pl.BlockSpec(memory_space=pltpu.HBM)


def partner_a(tile, tiles):
    other = tile ^ 1
    return other if other < tiles else tile


def partner_b(tile, tiles):
    other = ((tile - 1) ^ 1) + 1 if tile > 0 else tile
    return other if other < tiles else tile


def idle_cycle(where, names):
    for k, name in enumerate(names):
        where[name] = names[(k + 1) % len(names)]


def section_hop(layer, sections):
    where = {}
    if layer % 2 == 0:
        idle_cycle(where, [layer, layer + 1])
    elif layer + 2 < sections:
        idle_cycle(where, [layer - 1, layer, layer + 1, layer + 2])
    else:
        idle_cycle(where, [layer - 1, layer, layer + 1])
    taken = set(where)
    for s in range(sections):
        if s not in taken:
            where[s] = s ^ 1 if (s ^ 1) not in taken and (s ^ 1) < sections else s
    return where


def hop_pairs(layer, tiles, sections, tile_of):
    hop = section_hop(layer, sections)
    pairs = []
    for t in range(tiles):
        for s in range(sections):
            goal = tile_of(t) if s == layer else t
            pairs.append((t * sections + s, goal * sections + hop[s]))
    return pairs


def rim_pairs(tiles, sections, tile_of):
    pairs = []
    for t in range(tiles):
        where = {}
        if tile_of(t) == t:
            for s in range(sections):
                where[s] = s ^ 1 if (s ^ 1) < sections else s
        else:
            idle_cycle(where, list(range(1, sections)))
        for s in range(sections):
            if s == 0 and tile_of(t) != t:
                pairs.append((t * sections, tile_of(t) * sections))
            else:
                pairs.append((t * sections + s, t * sections + where[s]))
    return pairs


def share_pairs(target, tiles, sections):
    last = sections - 1
    where = {}
    if target == last - 1 or (target ^ 1) >= last - 1:
        idle_cycle(where, [last, target])
    else:
        idle_cycle(where, [last, target, target ^ 1, last - 1])
    taken = set(where)
    for s in range(sections):
        if s not in taken:
            where[s] = s ^ 1 if (s ^ 1) not in taken and (s ^ 1) < sections else s
    return [
        (t * sections + s, t * sections + where[s])
        for t in range(tiles)
        for s in range(sections)
    ]


def send(value, pairs):
    return lax.ppermute(value, ("tiles", "section"), pairs)


def split(values):
    high = values.astype(jnp.bfloat16)
    low = (values - high.astype(jnp.float32)).astype(jnp.bfloat16)
    return high, low


def held(shape, dtype=jnp.float32):
    return pltpu.VMEM(shape, dtype)


def prepare(weight, gain, steps, depth, width):
    channels = weight.shape[1]
    first = 9 * (3 - steps)
    groups = [(k, min(2, 9 - k)) for k in range(0, 9, 2)]

    def kernel(weight_ref, gain_ref, high, low, gains, staged, row, sems, gain_sem):
        gain_copy = pltpu.make_async_copy(gain_ref, row, gain_sem)
        gain_copy.start()
        copies = {}
        for a in reversed(range(steps)):
            for n, (k, size) in enumerate(groups):
                at = 9 * a + k
                copies[a, k] = pltpu.make_async_copy(
                    weight_ref.at[pl.ds(first + at, size)],
                    staged.at[pl.ds(at, size)],
                    sems.at[a, n],
                )
                copies[a, k].start()
        gain_copy.wait()
        square = (channels, channels)
        lane = lax.broadcasted_iota(jnp.int32, square, 1)
        sublane = lax.broadcasted_iota(jnp.int32, square, 0)
        spread = jnp.broadcast_to(row[...], square)
        column = jnp.sum(jnp.where(lane == sublane, spread, 0.0), axis=1, keepdims=True)
        gains[...] = jnp.broadcast_to(column, (channels, width))
        for a in reversed(range(steps)):
            for k, size in groups:
                copies[a, k].wait()
                parts = [staged[9 * a + k + n] for n in range(size)]
                span = size * channels
                if k + size == 9 and depth > 9 * channels:
                    extra = depth - 9 * channels
                    parts.append(jnp.zeros((channels, extra), jnp.float32))
                    span += extra
                upper, lower = split(jnp.concatenate(parts, axis=1))
                high[a, :, k * channels : k * channels + span] = upper
                low[a, :, k * channels : k * channels + span] = lower

    shape = (steps, channels, depth)
    return pl.pallas_call(
        kernel,
        out_shape=(
            held(shape, jnp.bfloat16),
            held(shape, jnp.bfloat16),
            held((channels, width)),
        ),
        in_specs=[HBM, HBM],
        out_specs=(VMEM, VMEM, VMEM),
        scratch_shapes=[
            pltpu.VMEM((9 * steps, channels, channels), jnp.float32),
            pltpu.VMEM(gain.shape, jnp.float32),
            pltpu.SemaphoreType.DMA((steps, len(groups))),
            pltpu.SemaphoreType.DMA,
        ],
        compiler_params=GRANT,
        name="prepare",
    )(
        pltpu.with_memory_space_constraint(weight, pltpu.HBM),
        pltpu.with_memory_space_constraint(gain, pltpu.HBM),
    )


def edges(latents, rows):
    frames, lines, width = latents.shape
    channels = lines // rows

    def kernel(ref, out_a, out_b):
        even = lax.rem(lax.axis_index("tiles"), 2) == 0
        for f in range(frames):
            top = ref[f, pl.ds(0, channels, stride=rows), :]
            bottom = ref[f, pl.ds(rows - 1, channels, stride=rows), :]
            out_a[f] = jnp.where(even, bottom, top)
            out_b[f] = jnp.where(even, top, bottom)

    return pl.pallas_call(
        kernel,
        out_shape=tuple([held((frames, channels, width))] * 2),
        in_specs=[VMEM],
        out_specs=(VMEM, VMEM),
        compiler_params=GRANT,
        name="edges",
    )(latents)


def normalize(values, gain):
    meansq = jnp.mean(values * values, axis=0, keepdims=True)
    scaled = values * lax.rsqrt(meansq + EPSILON) * gain
    return scaled / (1.0 + jnp.exp(-scaled))


def shifted(values, col_off):
    if col_off == 1:
        return values
    width = values.shape[1]
    lane = lax.broadcasted_iota(jnp.int32, values.shape, 1)
    if col_off == 0:
        return jnp.where(lane == 0, 0.0, pltpu.roll(values, 1, 1))
    return jnp.where(lane == width - 1, 0.0, pltpu.roll(values, width - 1, 1))


def product(high, low, patch_high, patch_low):
    def dot(a, b):
        return jnp.dot(a, b, preferred_element_type=jnp.float32)

    return dot(high, patch_high) + dot(low, patch_high) + dot(high, patch_low)


def frame_step(layer, tiles, sections, main, frame, near_a, near_b, gain, weights, partial, keep):
    channels, width = near_a.shape[-2:]
    lines = main.shape[-2]
    rows = lines // channels
    steps, _, depth = weights[0].shape
    last = layer == sections - 1
    share = lines // sections
    count = sections if last else 3

    def kernel(*refs):
        main_ref, a_ref, b_ref, gain_ref, high_ref, low_ref = refs[:6]
        refs = refs[6:]
        if partial is not None:
            partial_ref, refs = refs[0], refs[1:]
        outs, (patch_high, patch_low) = refs[:count], refs[count:]
        tile = lax.axis_index("tiles")
        even = lax.rem(tile, 2) == 0

        @pl.when(lax.axis_index("section") == layer)
        def _():
            gains = gain_ref[...]
            near_one, near_two = (
                ref[...] if frame is None else ref[frame] for ref in (a_ref, b_ref)
            )
            above = jnp.where(even, near_two, near_one)
            below = jnp.where(even, near_one, near_two)
            above = jnp.where(tile == 0, 0.0, above)
            below = jnp.where(tile == tiles - 1, 0.0, below)
            own = []
            for r in range(rows):
                line = pl.ds(r, channels, stride=rows)
                own.append(main_ref[line, :] if frame is None else main_ref[frame, line, :])
            if depth > 9 * channels:
                pad = jnp.zeros((depth - 9 * channels, rows * width), jnp.bfloat16)
                patch_high[9 * channels :, :] = pad
                patch_low[9 * channels :, :] = pad
            for q, source in enumerate([above] + own + [below]):
                normed = normalize(source, gains)
                for e in range(3):
                    upper, lower = split(shifted(normed, e))
                    for b in range(3):
                        r = q - b
                        if 0 <= r < rows:
                            k = (3 * b + e) * channels
                            cols = slice(r * width, (r + 1) * width)
                            patch_high[k : k + channels, cols] = upper
                            patch_low[k : k + channels, cols] = lower
            total = product(
                high_ref[steps - 1], low_ref[steps - 1], patch_high[...], patch_low[...]
            )
            if partial is not None:
                total = total + partial_ref[...]
            results = [
                own[r] + total[:, r * width : (r + 1) * width] for r in range(rows)
            ]
            if last:
                part = share // rows
                for s in range(sections):
                    for r in range(rows):
                        outs[s][pl.ds(r, part, stride=rows), :] = results[r][
                            s * part : (s + 1) * part
                        ]
            else:
                for r in range(rows):
                    outs[0][pl.ds(r, channels, stride=rows), :] = results[r]
                outs[1][...] = jnp.where(even, results[-1], results[0])
                outs[2][...] = jnp.where(even, results[0], results[-1])

    operands = [main, near_a, near_b, gain, *weights]
    if partial is not None:
        operands.append(partial)
    if last:
        out_shape = [held((share, width))] * sections
    else:
        edge = held((channels, width))
        out_shape = [held((lines, width)), edge, edge]
    patch = held((depth, rows * width), jnp.bfloat16)
    scratch = []
    if keep:
        out_shape += [patch, patch]
    else:
        scratch = [patch, patch]
    return pl.pallas_call(
        kernel,
        out_shape=tuple(out_shape),
        in_specs=[VMEM] * len(operands),
        out_specs=tuple([VMEM] * len(out_shape)),
        scratch_shapes=scratch,
        cost_estimate=pl.CostEstimate(
            flops=6 * channels * depth * rows * width,
            bytes_accessed=2**20,
            transcendentals=0,
        ),
        compiler_params=GRANT,
        name="frame_step",
    )(*operands)


def earlier_frames(layer, weights, patches):
    steps, channels, depth = weights[0].shape
    count = len(patches)
    columns = patches[0][0].shape[1]

    def kernel(high_ref, low_ref, *refs):
        out_ref = refs[-1]

        @pl.when(lax.axis_index("section") == layer)
        def _():
            total = None
            for n in range(count):
                a = steps - 1 - (count - n)
                term = product(
                    high_ref[a], low_ref[a], refs[2 * n][...], refs[2 * n + 1][...]
                )
                total = term if total is None else total + term
            out_ref[...] = total

    operands = [*weights]
    for pair in patches:
        operands += list(pair)
    return pl.pallas_call(
        kernel,
        out_shape=held((channels, columns)),
        in_specs=[VMEM] * len(operands),
        out_specs=VMEM,
        cost_estimate=pl.CostEstimate(
            flops=6 * channels * depth * columns * count,
            bytes_accessed=2**20,
            transcendentals=0,
        ),
        compiler_params=GRANT,
        name="earlier_frames",
    )(*operands)


def local(latents, conv_weight, gain):
    frames, channels, rows, width = latents.shape
    tiles, sections = lax.axis_size("tiles"), lax.axis_size("section")
    section = lax.axis_index("section")
    depth = -(-9 * channels // 256) * 256
    steps = min(frames, 3)
    of_a = lambda t: partner_a(t, tiles)
    of_b = lambda t: partner_b(t, tiles)

    flat = latents.reshape(frames, channels * rows, width)
    edge_a, edge_b = edges(flat, rows)
    rim_a, rim_b = (rim_pairs(tiles, sections, of) for of in (of_a, of_b))
    near_a = [send(edge_a, rim_a)] * frames
    near_b = [send(edge_b, rim_b)] * frames
    *weights, gains = prepare(conv_weight[0], gain, steps, depth, width)
    main = [flat] * frames

    for layer in range(sections):
        if layer > 0:
            straight = hop_pairs(layer - 1, tiles, sections, lambda t: t)
            cross_a = hop_pairs(layer - 1, tiles, sections, of_a)
            cross_b = hop_pairs(layer - 1, tiles, sections, of_b)
            main = [send(main[f], straight) for f in range(frames)]
            near_a = [send(edge_a[f], cross_a) for f in range(frames)]
            near_b = [send(edge_b[f], cross_b) for f in range(frames)]
        patches, next_main, edge_a, edge_b = [], [], [], []
        for f in range(frames):
            partial = None
            if f > 0:
                partial = earlier_frames(layer, weights, patches[-2:])
            keep = f < frames - 1
            done = frame_step(
                layer, tiles, sections, main[f], f if layer == 0 else None,
                near_a[f], near_b[f], gains, weights, partial, keep,
            )
            if keep:
                patches.append(done[-2:])
                done = done[:-2]
            next_main.append(done if layer == sections - 1 else done[0])
            edge_a.append(done[1])
            edge_b.append(done[2])
        main = next_main

    outs = []
    for f in range(frames):
        own = main[f][sections - 1]
        for target in range(sections - 1):
            pairs = share_pairs(target, tiles, sections)
            got = send(main[f][target], pairs)
            own = jnp.where(section == target, got, own)
        outs.append(own)
    return jnp.stack(outs).reshape(frames, channels // sections, rows, width)


def solution(mesh):
    return jax.shard_map(
        local,
        mesh=mesh,
        in_specs=(
            P("groups", None, "tiles", None),
            P("section", None, None, None),
            P("section", None),
        ),
        out_specs=P("groups", "section", "tiles", None),
        check_vma=False,
    )
```

```python
import jax
import jax.numpy as jnp
from jax import lax
from jax.experimental import pallas as pl
from jax.experimental.pallas import tpu as pltpu
from jax.sharding import PartitionSpec as P


EPSILON = 1e-06
GRANT = pltpu.CompilerParams(vmem_limit_bytes=12 * 2**20)
VMEM = pl.BlockSpec(memory_space=pltpu.VMEM)
HBM = pl.BlockSpec(memory_space=pltpu.HBM)


def partner_a(tile, tiles):
    other = tile ^ 1
    return other if other < tiles else tile


def partner_b(tile, tiles):
    other = ((tile - 1) ^ 1) + 1 if tile > 0 else tile
    return other if other < tiles else tile


def idle_cycle(where, names):
    for k, name in enumerate(names):
        where[name] = names[(k + 1) % len(names)]


def section_hop(layer, sections):
    where = {}
    if layer % 2 == 0:
        idle_cycle(where, [layer, layer + 1])
    elif layer + 2 < sections:
        idle_cycle(where, [layer - 1, layer, layer + 1, layer + 2])
    else:
        idle_cycle(where, [layer - 1, layer, layer + 1])
    taken = set(where)
    for s in range(sections):
        if s not in taken:
            where[s] = s ^ 1 if (s ^ 1) not in taken and (s ^ 1) < sections else s
    return where


def all_pairs(shape, goal):
    groups, tiles, sections = shape
    pairs = []
    for g in range(groups):
        for t in range(tiles):
            for s in range(sections):
                to_g, to_t, to_s = goal(g, t, s)
                pairs.append(
                    ((g * tiles + t) * sections + s, (to_g * tiles + to_t) * sections + to_s)
                )
    return pairs


def other_group(g, groups):
    return g ^ 1 if (g ^ 1) < groups else g


def hop_pairs(layer, shape, tile_of):
    hop = section_hop(layer, shape[2])
    return all_pairs(
        shape, lambda g, t, s: (g, tile_of(t) if s == layer else t, hop[s])
    )


def rim_pairs(shape, tile_of):
    groups, _, sections = shape

    def goal(g, t, s):
        if tile_of(t) == t and sections % 2 == 0:
            return g, t, s ^ 1
        if s == 0:
            return g, tile_of(t), s
        if s == 1 or s ^ 1 >= sections:
            return other_group(g, groups), t, s
        return g, t, s ^ 1

    return all_pairs(shape, goal)


def share_pairs(target, shape):
    groups, _, sections = shape
    last = sections - 1
    where = {}
    if target == last - 1 or target == 0:
        idle_cycle(where, [last, target])
    else:
        idle_cycle(where, [last, target, last - 1])

    def goal(g, t, s):
        if s in where:
            return g, t, where[s]
        if target == last - 1 and s ^ 1 < last - 1:
            return g, t, s ^ 1
        return other_group(g, groups), t, s

    return all_pairs(shape, goal)


def send(value, pairs):
    return lax.ppermute(value, ("groups", "tiles", "section"), pairs)


def split(values):
    high = values.astype(jnp.bfloat16)
    low = (values - high.astype(jnp.float32)).astype(jnp.bfloat16)
    return high, low


def held(shape, dtype=jnp.float32):
    return pltpu.VMEM(shape, dtype)


def prepare(weight, gain, steps, depth, width):
    channels = weight.shape[1]
    first = 9 * (3 - steps)
    groups = [(k, min(2, 9 - k)) for k in range(0, 9, 2)]

    def kernel(weight_ref, gain_ref, high, low, gains, staged, row, sems, gain_sem):
        gain_copy = pltpu.make_async_copy(gain_ref, row, gain_sem)
        gain_copy.start()
        copies = {}
        for a in reversed(range(steps)):
            for n, (k, size) in enumerate(groups):
                at = 9 * a + k
                copies[a, k] = pltpu.make_async_copy(
                    weight_ref.at[pl.ds(first + at, size)],
                    staged.at[pl.ds(at, size)],
                    sems.at[a, n],
                )
                copies[a, k].start()
        for a in reversed(range(steps)):
            for k, size in groups:
                copies[a, k].wait()
                parts = [staged[9 * a + k + n] for n in range(size)]
                span = size * channels
                if k + size == 9 and depth > 9 * channels:
                    extra = depth - 9 * channels
                    parts.append(jnp.zeros((channels, extra), jnp.float32))
                    span += extra
                upper, lower = split(jnp.concatenate(parts, axis=1))
                high[a, :, k * channels : k * channels + span] = upper
                low[a, :, k * channels : k * channels + span] = lower
        gain_copy.wait()
        square = (channels, channels)
        lane = lax.broadcasted_iota(jnp.int32, square, 1)
        sublane = lax.broadcasted_iota(jnp.int32, square, 0)
        spread = jnp.broadcast_to(row[...], square)
        column = jnp.sum(jnp.where(lane == sublane, spread, 0.0), axis=1, keepdims=True)
        gains[...] = jnp.broadcast_to(column, (channels, width))

    shape = (steps, channels, depth)
    return pl.pallas_call(
        kernel,
        out_shape=(
            held(shape, jnp.bfloat16),
            held(shape, jnp.bfloat16),
            held((channels, width)),
        ),
        in_specs=[HBM, HBM],
        out_specs=(VMEM, VMEM, VMEM),
        scratch_shapes=[
            pltpu.VMEM((9 * steps, channels, channels), jnp.float32),
            pltpu.VMEM(gain.shape, jnp.float32),
            pltpu.SemaphoreType.DMA((steps, len(groups))),
            pltpu.SemaphoreType.DMA,
        ],
        compiler_params=GRANT,
        name="prepare",
    )(
        pltpu.with_memory_space_constraint(weight, pltpu.HBM),
        pltpu.with_memory_space_constraint(gain, pltpu.HBM),
    )


def edges(latents, rows):
    frames, lines, width = latents.shape
    channels = lines // rows

    def kernel(ref, out_a, out_b):
        even = lax.rem(lax.axis_index("tiles"), 2) == 0
        for f in range(frames):
            top = ref[f, pl.ds(0, channels, stride=rows), :]
            bottom = ref[f, pl.ds(rows - 1, channels, stride=rows), :]
            out_a[f] = jnp.where(even, bottom, top)
            out_b[f] = jnp.where(even, top, bottom)

    return pl.pallas_call(
        kernel,
        out_shape=tuple([held((frames, channels, width))] * 2),
        in_specs=[VMEM],
        out_specs=(VMEM, VMEM),
        compiler_params=GRANT,
        name="edges",
    )(latents)


def normalize(values, gain):
    meansq = jnp.mean(values * values, axis=0, keepdims=True)
    scaled = values * lax.rsqrt(meansq + EPSILON) * gain
    return scaled / (1.0 + jnp.exp(-scaled))


def shifted(values, col_off):
    if col_off == 1:
        return values
    width = values.shape[1]
    lane = lax.broadcasted_iota(jnp.int32, values.shape, 1)
    if col_off == 0:
        return jnp.where(lane == 0, 0.0, pltpu.roll(values, 1, 1))
    return jnp.where(lane == width - 1, 0.0, pltpu.roll(values, width - 1, 1))


def product(high, low, patch_high, patch_low):
    def dot(a, b):
        return jnp.dot(a, b, preferred_element_type=jnp.float32)

    return dot(high, patch_high) + dot(low, patch_high) + dot(high, patch_low)


def frame_step(layer, tiles, sections, main, frame, near_a, near_b, gain, weights, partial, keep):
    channels, width = near_a.shape[-2:]
    lines = main.shape[-2]
    rows = lines // channels
    steps, _, depth = weights[0].shape
    last = layer == sections - 1
    share = lines // sections
    count = sections if last else 3

    def kernel(*refs):
        main_ref, a_ref, b_ref, gain_ref, high_ref, low_ref = refs[:6]
        refs = refs[6:]
        if partial is not None:
            partial_ref, refs = refs[0], refs[1:]
        outs, (patch_high, patch_low) = refs[:count], refs[count:]
        tile = lax.axis_index("tiles")
        even = lax.rem(tile, 2) == 0

        @pl.when(lax.axis_index("section") == layer)
        def _():
            gains = gain_ref[...]
            near_one, near_two = (
                ref[...] if frame is None else ref[frame] for ref in (a_ref, b_ref)
            )
            above = jnp.where(even, near_two, near_one)
            below = jnp.where(even, near_one, near_two)
            above = jnp.where(tile == 0, 0.0, above)
            below = jnp.where(tile == tiles - 1, 0.0, below)
            own = []
            for r in range(rows):
                line = pl.ds(r, channels, stride=rows)
                own.append(main_ref[line, :] if frame is None else main_ref[frame, line, :])
            if depth > 9 * channels:
                pad = jnp.zeros((depth - 9 * channels, rows * width), jnp.bfloat16)
                patch_high[9 * channels :, :] = pad
                patch_low[9 * channels :, :] = pad
            for q, source in enumerate([above] + own + [below]):
                normed = normalize(source, gains)
                for e in range(3):
                    upper, lower = split(shifted(normed, e))
                    for b in range(3):
                        r = q - b
                        if 0 <= r < rows:
                            k = (3 * b + e) * channels
                            cols = slice(r * width, (r + 1) * width)
                            patch_high[k : k + channels, cols] = upper
                            patch_low[k : k + channels, cols] = lower
            total = product(
                high_ref[steps - 1], low_ref[steps - 1], patch_high[...], patch_low[...]
            )
            if partial is not None:
                total = total + partial_ref[...]
            results = [
                own[r] + total[:, r * width : (r + 1) * width] for r in range(rows)
            ]
            if last:
                part = share // rows
                for s in range(sections):
                    for r in range(rows):
                        outs[s][pl.ds(r, part, stride=rows), :] = results[r][
                            s * part : (s + 1) * part
                        ]
            else:
                for r in range(rows):
                    outs[0][pl.ds(r, channels, stride=rows), :] = results[r]
                outs[1][...] = jnp.where(even, results[-1], results[0])
                outs[2][...] = jnp.where(even, results[0], results[-1])

    operands = [main, near_a, near_b, gain, *weights]
    if partial is not None:
        operands.append(partial)
    if last:
        out_shape = [held((share, width))] * sections
    else:
        edge = held((channels, width))
        out_shape = [held((lines, width)), edge, edge]
    patch = held((depth, rows * width), jnp.bfloat16)
    scratch = []
    if keep:
        out_shape += [patch, patch]
    else:
        scratch = [patch, patch]
    return pl.pallas_call(
        kernel,
        out_shape=tuple(out_shape),
        in_specs=[VMEM] * len(operands),
        out_specs=tuple([VMEM] * len(out_shape)),
        scratch_shapes=scratch,
        cost_estimate=pl.CostEstimate(
            flops=6 * channels * depth * rows * width,
            bytes_accessed=2**20,
            transcendentals=0,
        ),
        compiler_params=GRANT,
        name="frame_step",
    )(*operands)


def earlier_frames(layer, weights, patches):
    steps, channels, depth = weights[0].shape
    count = len(patches)
    columns = patches[0][0].shape[1]

    def kernel(high_ref, low_ref, *refs):
        out_ref = refs[-1]

        @pl.when(lax.axis_index("section") == layer)
        def _():
            total = None
            for n in range(count):
                a = steps - 1 - (count - n)
                term = product(
                    high_ref[a], low_ref[a], refs[2 * n][...], refs[2 * n + 1][...]
                )
                total = term if total is None else total + term
            out_ref[...] = total

    operands = [*weights]
    for pair in patches:
        operands += list(pair)
    return pl.pallas_call(
        kernel,
        out_shape=held((channels, columns)),
        in_specs=[VMEM] * len(operands),
        out_specs=VMEM,
        cost_estimate=pl.CostEstimate(
            flops=6 * channels * depth * columns * count,
            bytes_accessed=2**20,
            transcendentals=0,
        ),
        compiler_params=GRANT,
        name="earlier_frames",
    )(*operands)


def local(latents, conv_weight, gain):
    frames, channels, rows, width = latents.shape
    tiles, sections = lax.axis_size("tiles"), lax.axis_size("section")
    shape = (lax.axis_size("groups"), tiles, sections)
    depth = -(-9 * channels // 256) * 256
    steps = min(frames, 3)
    of_a = lambda t: partner_a(t, tiles)
    of_b = lambda t: partner_b(t, tiles)

    flat = latents.reshape(frames, channels * rows, width)
    edge_a, edge_b = edges(flat, rows)
    rim_a, rim_b = (rim_pairs(shape, of) for of in (of_a, of_b))
    near_a = [send(edge_a, rim_a)] * frames
    near_b = [send(edge_b, rim_b)] * frames
    *weights, gains = prepare(conv_weight[0], gain, steps, depth, width)
    main = [flat] * frames

    for layer in range(sections):
        if layer > 0:
            straight = hop_pairs(layer - 1, shape, lambda t: t)
            cross_a = hop_pairs(layer - 1, shape, of_a)
            cross_b = hop_pairs(layer - 1, shape, of_b)
            main = [send(main[f], straight) for f in range(frames)]
            near_a = [send(edge_a[f], cross_a) for f in range(frames)]
            near_b = [send(edge_b[f], cross_b) for f in range(frames)]
        patches, next_main, edge_a, edge_b = [], [], [], []
        for f in range(frames):
            partial = None
            if f > 0:
                partial = earlier_frames(layer, weights, patches[-2:])
            keep = f < frames - 1
            done = frame_step(
                layer, tiles, sections, main[f], f if layer == 0 else None,
                near_a[f], near_b[f], gains, weights, partial, keep,
            )
            if keep:
                patches.append(done[-2:])
                done = done[:-2]
            next_main.append(done if layer == sections - 1 else done[0])
            edge_a.append(done[1])
            edge_b.append(done[2])
        main = next_main

    parts = []
    for f in range(frames):
        for target in range(sections - 1):
            pairs = share_pairs(target, shape)
            parts.append(send(main[f][target], pairs))
        parts.append(main[f][sections - 1])
    return assemble(parts, frames, sections).reshape(
        frames, channels // sections, rows, width
    )


def assemble(parts, frames, sections):
    lines, width = parts[0].shape

    def kernel(*refs):
        out = refs[-1]
        for s in range(sections):

            @pl.when(lax.axis_index("section") == s)
            def _():
                for f in range(frames):
                    out[f] = refs[f * sections + s][...]

    return pl.pallas_call(
        kernel,
        out_shape=jax.ShapeDtypeStruct((frames, lines, width), jnp.float32),
        in_specs=[VMEM] * len(parts),
        out_specs=VMEM,
        compiler_params=GRANT,
        name="assemble",
    )(*parts)


def solution(mesh):
    return jax.shard_map(
        local,
        mesh=mesh,
        in_specs=(
            P("groups", None, "tiles", None),
            P("section", None, None, None),
            P("section", None),
        ),
        out_specs=P("groups", "section", "tiles", None),
        check_vma=False,
    )
```

```python
import jax
import jax.numpy as jnp
from jax import lax
from jax.experimental import pallas as pl
from jax.experimental.pallas import tpu as pltpu
from jax.sharding import PartitionSpec as P


EPSILON = 1e-06
GRANT = pltpu.CompilerParams(vmem_limit_bytes=12 * 2**20)
VMEM = pl.BlockSpec(memory_space=pltpu.VMEM)
HBM = pl.BlockSpec(memory_space=pltpu.HBM)


def partner_a(tile, tiles):
    other = tile ^ 1
    return other if other < tiles else tile


def partner_b(tile, tiles):
    other = ((tile - 1) ^ 1) + 1 if tile > 0 else tile
    return other if other < tiles else tile


def idle_cycle(where, names):
    for k, name in enumerate(names):
        where[name] = names[(k + 1) % len(names)]


def section_hop(layer, sections):
    where = {}
    if layer % 2 == 0:
        idle_cycle(where, [layer, layer + 1])
    elif layer + 2 < sections:
        idle_cycle(where, [layer - 1, layer, layer + 1, layer + 2])
    else:
        idle_cycle(where, [layer - 1, layer, layer + 1])
    taken = set(where)
    for s in range(sections):
        if s not in taken:
            where[s] = s ^ 1 if (s ^ 1) not in taken and (s ^ 1) < sections else s
    return where


def all_pairs(shape, goal):
    groups, tiles, sections = shape
    pairs = []
    for g in range(groups):
        for t in range(tiles):
            for s in range(sections):
                to_g, to_t, to_s = goal(g, t, s)
                pairs.append(
                    ((g * tiles + t) * sections + s, (to_g * tiles + to_t) * sections + to_s)
                )
    return pairs


def other_group(g, groups):
    return g ^ 1 if (g ^ 1) < groups else g


def hop_pairs(layer, shape, tile_of):
    hop = section_hop(layer, shape[2])
    return all_pairs(
        shape, lambda g, t, s: (g, tile_of(t) if s == layer else t, hop[s])
    )


def rim_pairs(shape, tile_of):
    groups, _, sections = shape

    def goal(g, t, s):
        if tile_of(t) == t and sections % 2 == 0:
            return g, t, s ^ 1
        if s == 0:
            return g, tile_of(t), s
        if s == 1 or s ^ 1 >= sections:
            return other_group(g, groups), t, s
        return g, t, s ^ 1

    return all_pairs(shape, goal)


def share_pairs(target, shape):
    groups, _, sections = shape
    last = sections - 1
    where = {}
    if target == last - 1:
        idle_cycle(where, [last, target])
    elif target == 0:
        idle_cycle(where, [last, 0, 1, last - 1])
    else:
        idle_cycle(where, [last, target, target ^ 1])

    def goal(g, t, s):
        if s in where:
            return g, t, where[s]
        if s ^ 1 not in where and s ^ 1 < sections:
            return g, t, s ^ 1
        return other_group(g, groups), t, s

    return all_pairs(shape, goal)


def send(value, pairs):
    return lax.ppermute(value, ("groups", "tiles", "section"), pairs)


def split(values):
    high = values.astype(jnp.bfloat16)
    low = (values - high.astype(jnp.float32)).astype(jnp.bfloat16)
    return high, low


def held(shape, dtype=jnp.float32):
    return pltpu.VMEM(shape, dtype)


def prepare(weight, gain, steps, depth, width):
    channels = weight.shape[1]
    first = 9 * (3 - steps)
    groups = [(k, min(2, 9 - k)) for k in range(0, 9, 2)]

    def kernel(weight_ref, gain_ref, high, low, gains, staged, row, sems, gain_sem):
        gain_copy = pltpu.make_async_copy(gain_ref, row, gain_sem)
        gain_copy.start()
        copies = {}
        for a in reversed(range(steps)):
            for n, (k, size) in enumerate(groups):
                at = 9 * a + k
                copies[a, k] = pltpu.make_async_copy(
                    weight_ref.at[pl.ds(first + at, size)],
                    staged.at[pl.ds(at, size)],
                    sems.at[a, n],
                )
                copies[a, k].start()
        for a in reversed(range(steps)):
            for k, size in groups:
                copies[a, k].wait()
                parts = [staged[9 * a + k + n] for n in range(size)]
                span = size * channels
                if k + size == 9 and depth > 9 * channels:
                    extra = depth - 9 * channels
                    parts.append(jnp.zeros((channels, extra), jnp.float32))
                    span += extra
                upper, lower = split(jnp.concatenate(parts, axis=1))
                high[a, :, k * channels : k * channels + span] = upper
                low[a, :, k * channels : k * channels + span] = lower
        gain_copy.wait()
        square = (channels, channels)
        lane = lax.broadcasted_iota(jnp.int32, square, 1)
        sublane = lax.broadcasted_iota(jnp.int32, square, 0)
        spread = jnp.broadcast_to(row[...], square)
        column = jnp.sum(jnp.where(lane == sublane, spread, 0.0), axis=1, keepdims=True)
        gains[...] = jnp.broadcast_to(column, (channels, width))

    shape = (steps, channels, depth)
    return pl.pallas_call(
        kernel,
        out_shape=(
            held(shape, jnp.bfloat16),
            held(shape, jnp.bfloat16),
            held((channels, width)),
        ),
        in_specs=[HBM, HBM],
        out_specs=(VMEM, VMEM, VMEM),
        scratch_shapes=[
            pltpu.VMEM((9 * steps, channels, channels), jnp.float32),
            pltpu.VMEM(gain.shape, jnp.float32),
            pltpu.SemaphoreType.DMA((steps, len(groups))),
            pltpu.SemaphoreType.DMA,
        ],
        compiler_params=GRANT,
        name="prepare",
    )(
        pltpu.with_memory_space_constraint(weight, pltpu.HBM),
        pltpu.with_memory_space_constraint(gain, pltpu.HBM),
    )


def edges(latents, rows):
    frames, lines, width = latents.shape
    channels = lines // rows

    def kernel(ref, *outs):
        even = lax.rem(lax.axis_index("tiles"), 2) == 0
        for f in range(frames):
            top = ref[f, pl.ds(0, channels, stride=rows), :]
            bottom = ref[f, pl.ds(rows - 1, channels, stride=rows), :]
            outs[2 * f][...] = jnp.where(even, bottom, top)
            outs[2 * f + 1][...] = jnp.where(even, top, bottom)

    return pl.pallas_call(
        kernel,
        out_shape=tuple([held((channels, width))] * (2 * frames)),
        in_specs=[VMEM],
        out_specs=tuple([VMEM] * (2 * frames)),
        compiler_params=GRANT,
        name="edges",
    )(latents)


def normalize(values, gain):
    meansq = jnp.mean(values * values, axis=0, keepdims=True)
    scaled = values * lax.rsqrt(meansq + EPSILON) * gain
    return scaled / (1.0 + jnp.exp(-scaled))


def shifted(values, col_off):
    if col_off == 1:
        return values
    width = values.shape[1]
    lane = lax.broadcasted_iota(jnp.int32, values.shape, 1)
    if col_off == 0:
        return jnp.where(lane == 0, 0.0, pltpu.roll(values, 1, 1))
    return jnp.where(lane == width - 1, 0.0, pltpu.roll(values, width - 1, 1))


def product(high, low, patch_high, patch_low):
    def dot(a, b):
        return jnp.dot(a, b, preferred_element_type=jnp.float32)

    return dot(high, patch_high) + dot(low, patch_high) + dot(high, patch_low)


def frame_step(layer, tiles, sections, main, frame, near_a, near_b, gain, weights, partial, keep):
    channels, width = near_a.shape[-2:]
    lines = main.shape[-2]
    rows = lines // channels
    steps, _, depth = weights[0].shape
    last = layer == sections - 1
    share = lines // sections
    count = sections if last else 3

    def kernel(*refs):
        main_ref, a_ref, b_ref, gain_ref, high_ref, low_ref = refs[:6]
        refs = refs[6:]
        if partial is not None:
            partial_ref, refs = refs[0], refs[1:]
        outs, (patch_high, patch_low) = refs[:count], refs[count:]
        tile = lax.axis_index("tiles")
        even = lax.rem(tile, 2) == 0

        @pl.when(lax.axis_index("section") == layer)
        def _():
            gains = gain_ref[...]
            near_one, near_two = a_ref[...], b_ref[...]
            above = jnp.where(even, near_two, near_one)
            below = jnp.where(even, near_one, near_two)
            above = jnp.where(tile == 0, 0.0, above)
            below = jnp.where(tile == tiles - 1, 0.0, below)
            own = []
            for r in range(rows):
                line = pl.ds(r, channels, stride=rows)
                own.append(main_ref[line, :] if frame is None else main_ref[frame, line, :])
            if depth > 9 * channels:
                pad = jnp.zeros((depth - 9 * channels, rows * width), jnp.bfloat16)
                patch_high[9 * channels :, :] = pad
                patch_low[9 * channels :, :] = pad
            for q, source in enumerate([above] + own + [below]):
                normed = normalize(source, gains)
                for e in range(3):
                    upper, lower = split(shifted(normed, e))
                    for b in range(3):
                        r = q - b
                        if 0 <= r < rows:
                            k = (3 * b + e) * channels
                            cols = slice(r * width, (r + 1) * width)
                            patch_high[k : k + channels, cols] = upper
                            patch_low[k : k + channels, cols] = lower
            total = product(
                high_ref[steps - 1], low_ref[steps - 1], patch_high[...], patch_low[...]
            )
            if partial is not None:
                total = total + partial_ref[...]
            results = [
                own[r] + total[:, r * width : (r + 1) * width] for r in range(rows)
            ]
            if last:
                part = share // rows
                for s in range(sections):
                    for r in range(rows):
                        outs[s][pl.ds(r, part, stride=rows), :] = results[r][
                            s * part : (s + 1) * part
                        ]
            else:
                for r in range(rows):
                    outs[0][pl.ds(r, channels, stride=rows), :] = results[r]
                outs[1][...] = jnp.where(even, results[-1], results[0])
                outs[2][...] = jnp.where(even, results[0], results[-1])

    operands = [main, near_a, near_b, gain, *weights]
    if partial is not None:
        operands.append(partial)
    if last:
        out_shape = [held((share, width))] * sections
    else:
        edge = held((channels, width))
        out_shape = [held((lines, width)), edge, edge]
    patch = held((depth, rows * width), jnp.bfloat16)
    scratch = []
    if keep:
        out_shape += [patch, patch]
    else:
        scratch = [patch, patch]
    return pl.pallas_call(
        kernel,
        out_shape=tuple(out_shape),
        in_specs=[VMEM] * len(operands),
        out_specs=tuple([VMEM] * len(out_shape)),
        scratch_shapes=scratch,
        cost_estimate=pl.CostEstimate(
            flops=6 * channels * depth * rows * width,
            bytes_accessed=2**20,
            transcendentals=0,
        ),
        compiler_params=GRANT,
        name="frame_step",
    )(*operands)


def earlier_frames(layer, weights, patches):
    steps, channels, depth = weights[0].shape
    count = len(patches)
    columns = patches[0][0].shape[1]

    def kernel(high_ref, low_ref, *refs):
        out_ref = refs[-1]

        @pl.when(lax.axis_index("section") == layer)
        def _():
            total = None
            for n in range(count):
                a = steps - 1 - (count - n)
                term = product(
                    high_ref[a], low_ref[a], refs[2 * n][...], refs[2 * n + 1][...]
                )
                total = term if total is None else total + term
            out_ref[...] = total

    operands = [*weights]
    for pair in patches:
        operands += list(pair)
    return pl.pallas_call(
        kernel,
        out_shape=held((channels, columns)),
        in_specs=[VMEM] * len(operands),
        out_specs=VMEM,
        cost_estimate=pl.CostEstimate(
            flops=6 * channels * depth * columns * count,
            bytes_accessed=2**20,
            transcendentals=0,
        ),
        compiler_params=GRANT,
        name="earlier_frames",
    )(*operands)


def local(latents, conv_weight, gain):
    frames, channels, rows, width = latents.shape
    tiles, sections = lax.axis_size("tiles"), lax.axis_size("section")
    shape = (lax.axis_size("groups"), tiles, sections)
    depth = -(-9 * channels // 256) * 256
    steps = min(frames, 3)
    of_a = lambda t: partner_a(t, tiles)
    of_b = lambda t: partner_b(t, tiles)

    flat = latents.reshape(frames, channels * rows, width)
    edge = edges(flat, rows)
    edge_a, edge_b = edge[0::2], edge[1::2]
    rim_a, rim_b = (rim_pairs(shape, of) for of in (of_a, of_b))
    near_a = [send(edge_a[f], rim_a) for f in range(frames)]
    near_b = [send(edge_b[f], rim_b) for f in range(frames)]
    *weights, gains = prepare(conv_weight[0], gain, steps, depth, width)
    main = [flat] * frames

    for layer in range(sections):
        if layer > 0:
            straight = hop_pairs(layer - 1, shape, lambda t: t)
            cross_a = hop_pairs(layer - 1, shape, of_a)
            cross_b = hop_pairs(layer - 1, shape, of_b)
            main = [send(main[f], straight) for f in range(frames)]
            near_a = [send(edge_a[f], cross_a) for f in range(frames)]
            near_b = [send(edge_b[f], cross_b) for f in range(frames)]
        patches, next_main, edge_a, edge_b = [], [], [], []
        for f in range(frames):
            partial = None
            if f > 0:
                partial = earlier_frames(layer, weights, patches[-2:])
            keep = f < frames - 1
            done = frame_step(
                layer, tiles, sections, main[f], f if layer == 0 else None,
                near_a[f], near_b[f], gains, weights, partial, keep,
            )
            if keep:
                patches.append(done[-2:])
                done = done[:-2]
            next_main.append(done if layer == sections - 1 else done[0])
            edge_a.append(done[1])
            edge_b.append(done[2])
        main = next_main

    parts = []
    for f in range(frames):
        for target in range(sections - 1):
            pairs = share_pairs(target, shape)
            parts.append(send(main[f][target], pairs))
        parts.append(main[f][sections - 1])
    return assemble(parts, frames, sections).reshape(
        frames, channels // sections, rows, width
    )


def assemble(parts, frames, sections):
    lines, width = parts[0].shape

    def kernel(*refs):
        out = refs[-1]
        for s in range(sections):

            @pl.when(lax.axis_index("section") == s)
            def _():
                for f in range(frames):
                    out[f] = refs[f * sections + s][...]

    return pl.pallas_call(
        kernel,
        out_shape=jax.ShapeDtypeStruct((frames, lines, width), jnp.float32),
        in_specs=[VMEM] * len(parts),
        out_specs=VMEM,
        compiler_params=GRANT,
        name="assemble",
    )(*parts)


def solution(mesh):
    return jax.shard_map(
        local,
        mesh=mesh,
        in_specs=(
            P("groups", None, "tiles", None),
            P("section", None, None, None),
            P("section", None),
        ),
        out_specs=P("groups", "section", "tiles", None),
        check_vma=False,
    )
```

```python
import jax
import jax.numpy as jnp
from jax import lax
from jax.experimental import pallas as pl
from jax.experimental.pallas import tpu as pltpu
from jax.sharding import PartitionSpec as P


EPSILON = 1e-06
GRANT = pltpu.CompilerParams(vmem_limit_bytes=12 * 2**20)
VMEM = pl.BlockSpec(memory_space=pltpu.VMEM)
HBM = pl.BlockSpec(memory_space=pltpu.HBM)


def partner_a(tile, tiles):
    other = tile ^ 1
    return other if other < tiles else tile


def partner_b(tile, tiles):
    other = ((tile - 1) ^ 1) + 1 if tile > 0 else tile
    return other if other < tiles else tile


def idle_cycle(where, names):
    for k, name in enumerate(names):
        where[name] = names[(k + 1) % len(names)]


def section_hop(layer, sections):
    where = {}
    if layer % 2 == 0:
        idle_cycle(where, [layer, layer + 1])
    elif layer + 2 < sections:
        idle_cycle(where, [layer - 1, layer, layer + 1, layer + 2])
    else:
        idle_cycle(where, [layer - 1, layer, layer + 1])
    taken = set(where)
    for s in range(sections):
        if s not in taken:
            where[s] = s ^ 1 if (s ^ 1) not in taken and (s ^ 1) < sections else s
    return where


def all_pairs(shape, goal):
    groups, tiles, sections = shape
    pairs = []
    for g in range(groups):
        for t in range(tiles):
            for s in range(sections):
                to_g, to_t, to_s = goal(g, t, s)
                pairs.append(
                    ((g * tiles + t) * sections + s, (to_g * tiles + to_t) * sections + to_s)
                )
    return pairs


def other_group(g, groups):
    return g ^ 1 if (g ^ 1) < groups else g


def hop_pairs(layer, shape, tile_of):
    hop = section_hop(layer, shape[2])
    return all_pairs(
        shape, lambda g, t, s: (g, tile_of(t) if s == layer else t, hop[s])
    )


def rim_pairs(shape, tile_of):
    groups, _, sections = shape

    def goal(g, t, s):
        if tile_of(t) == t and sections % 2 == 0:
            return g, t, s ^ 1
        if s == 0:
            return g, tile_of(t), s
        if s == 1 or s ^ 1 >= sections:
            return other_group(g, groups), t, s
        return g, t, s ^ 1

    return all_pairs(shape, goal)


def share_pairs(target, shape):
    groups, _, sections = shape
    last = sections - 1
    where = {}
    if target == last - 1:
        idle_cycle(where, [last, target])
    elif target == 0:
        idle_cycle(where, [last, 0, 1, last - 1])
    else:
        idle_cycle(where, [last, target, target ^ 1])

    def goal(g, t, s):
        if s in where:
            return g, t, where[s]
        if s ^ 1 not in where and s ^ 1 < sections:
            return g, t, s ^ 1
        return other_group(g, groups), t, s

    return all_pairs(shape, goal)


def send(value, pairs):
    return lax.ppermute(value, ("groups", "tiles", "section"), pairs)


def split(values):
    high = values.astype(jnp.bfloat16)
    low = (values - high.astype(jnp.float32)).astype(jnp.bfloat16)
    return high, low


def held(shape, dtype=jnp.float32):
    return pltpu.VMEM(shape, dtype)


def prepare(weight, gain, steps, depth, width):
    channels = weight.shape[1]
    first = 9 * (3 - steps)
    groups = [(k, min(2, 9 - k)) for k in range(0, 9, 2)]

    def kernel(weight_ref, gain_ref, both, gains, staged, row, sems, gain_sem):
        gain_copy = pltpu.make_async_copy(gain_ref, row, gain_sem)
        gain_copy.start()
        copies = {}
        for a in reversed(range(steps)):
            for n, (k, size) in enumerate(groups):
                at = 9 * a + k
                copies[a, k] = pltpu.make_async_copy(
                    weight_ref.at[pl.ds(first + at, size)],
                    staged.at[pl.ds(at, size)],
                    sems.at[a, n],
                )
                copies[a, k].start()
        for a in reversed(range(steps)):
            for k, size in groups:
                copies[a, k].wait()
                parts = [staged[9 * a + k + n] for n in range(size)]
                span = size * channels
                if k + size == 9 and depth > 9 * channels:
                    extra = depth - 9 * channels
                    parts.append(jnp.zeros((channels, extra), jnp.float32))
                    span += extra
                upper, lower = split(jnp.concatenate(parts, axis=1))
                cols = slice(k * channels, k * channels + span)
                both[a, :channels, cols] = upper
                both[a, channels:, cols] = lower
        gain_copy.wait()
        square = (channels, channels)
        lane = lax.broadcasted_iota(jnp.int32, square, 1)
        sublane = lax.broadcasted_iota(jnp.int32, square, 0)
        spread = jnp.broadcast_to(row[...], square)
        column = jnp.sum(jnp.where(lane == sublane, spread, 0.0), axis=1, keepdims=True)
        gains[...] = jnp.broadcast_to(column, (channels, width))

    shape = (steps, 2 * channels, depth)
    return pl.pallas_call(
        kernel,
        out_shape=(
            held(shape, jnp.bfloat16),
            held((channels, width)),
        ),
        in_specs=[HBM, HBM],
        out_specs=(VMEM, VMEM),
        scratch_shapes=[
            pltpu.VMEM((9 * steps, channels, channels), jnp.float32),
            pltpu.VMEM(gain.shape, jnp.float32),
            pltpu.SemaphoreType.DMA((steps, len(groups))),
            pltpu.SemaphoreType.DMA,
        ],
        compiler_params=GRANT,
        name="prepare",
    )(
        pltpu.with_memory_space_constraint(weight, pltpu.HBM),
        pltpu.with_memory_space_constraint(gain, pltpu.HBM),
    )


def edges(latents, rows):
    frames, lines, width = latents.shape
    channels = lines // rows

    def kernel(ref, *outs):
        even = lax.rem(lax.axis_index("tiles"), 2) == 0
        for f in range(frames):
            top = ref[f, pl.ds(0, channels, stride=rows), :]
            bottom = ref[f, pl.ds(rows - 1, channels, stride=rows), :]
            outs[2 * f][...] = jnp.where(even, bottom, top)
            outs[2 * f + 1][...] = jnp.where(even, top, bottom)

    return pl.pallas_call(
        kernel,
        out_shape=tuple([held((channels, width))] * (2 * frames)),
        in_specs=[VMEM],
        out_specs=tuple([VMEM] * (2 * frames)),
        compiler_params=GRANT,
        name="edges",
    )(latents)


def normalize(values, gain):
    meansq = jnp.mean(values * values, axis=0, keepdims=True)
    scaled = values * lax.rsqrt(meansq + EPSILON) * gain
    return scaled / (1.0 + jnp.exp(-scaled))


def shifted(values, col_off):
    if col_off == 1:
        return values
    width = values.shape[1]
    lane = lax.broadcasted_iota(jnp.int32, values.shape, 1)
    if col_off == 0:
        return jnp.where(lane == 0, 0.0, pltpu.roll(values, 1, 1))
    return jnp.where(lane == width - 1, 0.0, pltpu.roll(values, width - 1, 1))


def product(both, patch_high, patch_low):
    def dot(a, b):
        return jnp.dot(a, b, preferred_element_type=jnp.float32)

    channels = both.shape[0] // 2
    first = dot(both, patch_high)
    return first[:channels] + first[channels:] + dot(both[:channels], patch_low)


def frame_step(layer, tiles, sections, main, frame, near_a, near_b, gain, weights, partial, keep):
    channels, width = near_a.shape[-2:]
    lines = main.shape[-2]
    rows = lines // channels
    steps, _, depth = weights.shape
    last = layer == sections - 1
    share = lines // sections
    count = sections if last else 3

    def kernel(*refs):
        main_ref, a_ref, b_ref, gain_ref, both_ref = refs[:5]
        refs = refs[5:]
        if partial is not None:
            partial_ref, refs = refs[0], refs[1:]
        outs, (patch_high, patch_low) = refs[:count], refs[count:]
        tile = lax.axis_index("tiles")
        even = lax.rem(tile, 2) == 0

        @pl.when(lax.axis_index("section") == layer)
        def _():
            gains = gain_ref[...]
            near_one, near_two = a_ref[...], b_ref[...]
            above = jnp.where(even, near_two, near_one)
            below = jnp.where(even, near_one, near_two)
            above = jnp.where(tile == 0, 0.0, above)
            below = jnp.where(tile == tiles - 1, 0.0, below)
            own = []
            for r in range(rows):
                line = pl.ds(r, channels, stride=rows)
                own.append(main_ref[line, :] if frame is None else main_ref[frame, line, :])
            if depth > 9 * channels:
                pad = jnp.zeros((depth - 9 * channels, rows * width), jnp.bfloat16)
                patch_high[9 * channels :, :] = pad
                patch_low[9 * channels :, :] = pad
            for q, source in enumerate([above] + own + [below]):
                normed = normalize(source, gains)
                for e in range(3):
                    upper, lower = split(shifted(normed, e))
                    for b in range(3):
                        r = q - b
                        if 0 <= r < rows:
                            k = (3 * b + e) * channels
                            cols = slice(r * width, (r + 1) * width)
                            patch_high[k : k + channels, cols] = upper
                            patch_low[k : k + channels, cols] = lower
            total = product(both_ref[steps - 1], patch_high[...], patch_low[...])
            if partial is not None:
                total = total + partial_ref[...]
            results = [
                own[r] + total[:, r * width : (r + 1) * width] for r in range(rows)
            ]
            if last:
                part = share // rows
                for s in range(sections):
                    for r in range(rows):
                        outs[s][pl.ds(r, part, stride=rows), :] = results[r][
                            s * part : (s + 1) * part
                        ]
            else:
                for r in range(rows):
                    outs[0][pl.ds(r, channels, stride=rows), :] = results[r]
                outs[1][...] = jnp.where(even, results[-1], results[0])
                outs[2][...] = jnp.where(even, results[0], results[-1])

    operands = [main, near_a, near_b, gain, weights]
    if partial is not None:
        operands.append(partial)
    if last:
        out_shape = [held((share, width))] * sections
    else:
        edge = held((channels, width))
        out_shape = [held((lines, width)), edge, edge]
    patch = held((depth, rows * width), jnp.bfloat16)
    scratch = []
    if keep:
        out_shape += [patch, patch]
    else:
        scratch = [patch, patch]
    return pl.pallas_call(
        kernel,
        out_shape=tuple(out_shape),
        in_specs=[VMEM] * len(operands),
        out_specs=tuple([VMEM] * len(out_shape)),
        scratch_shapes=scratch,
        cost_estimate=pl.CostEstimate(
            flops=6 * channels * depth * rows * width,
            bytes_accessed=2**20,
            transcendentals=0,
        ),
        compiler_params=GRANT,
        name="frame_step",
    )(*operands)


def earlier_frames(layer, weights, patches):
    steps, channels, depth = weights.shape[0], weights.shape[1] // 2, weights.shape[2]
    count = len(patches)
    columns = patches[0][0].shape[1]

    def kernel(both_ref, *refs):
        out_ref = refs[-1]

        @pl.when(lax.axis_index("section") == layer)
        def _():
            total = None
            for n in range(count):
                a = steps - 1 - (count - n)
                term = product(both_ref[a], refs[2 * n][...], refs[2 * n + 1][...])
                total = term if total is None else total + term
            out_ref[...] = total

    operands = [weights]
    for pair in patches:
        operands += list(pair)
    return pl.pallas_call(
        kernel,
        out_shape=held((channels, columns)),
        in_specs=[VMEM] * len(operands),
        out_specs=VMEM,
        cost_estimate=pl.CostEstimate(
            flops=6 * channels * depth * columns * count,
            bytes_accessed=2**20,
            transcendentals=0,
        ),
        compiler_params=GRANT,
        name="earlier_frames",
    )(*operands)


def local(latents, conv_weight, gain):
    frames, channels, rows, width = latents.shape
    tiles, sections = lax.axis_size("tiles"), lax.axis_size("section")
    shape = (lax.axis_size("groups"), tiles, sections)
    depth = -(-9 * channels // 256) * 256
    steps = min(frames, 3)
    of_a = lambda t: partner_a(t, tiles)
    of_b = lambda t: partner_b(t, tiles)

    flat = latents.reshape(frames, channels * rows, width)
    edge = edges(flat, rows)
    edge_a, edge_b = edge[0::2], edge[1::2]
    rim_a, rim_b = (rim_pairs(shape, of) for of in (of_a, of_b))
    near_a = [send(edge_a[f], rim_a) for f in range(frames)]
    near_b = [send(edge_b[f], rim_b) for f in range(frames)]
    weights, gains = prepare(conv_weight[0], gain, steps, depth, width)
    main = [flat] * frames

    for layer in range(sections):
        if layer > 0:
            straight = hop_pairs(layer - 1, shape, lambda t: t)
            cross_a = hop_pairs(layer - 1, shape, of_a)
            cross_b = hop_pairs(layer - 1, shape, of_b)
            main = [send(main[f], straight) for f in range(frames)]
            near_a = [send(edge_a[f], cross_a) for f in range(frames)]
            near_b = [send(edge_b[f], cross_b) for f in range(frames)]
        patches, next_main, edge_a, edge_b = [], [], [], []
        for f in range(frames):
            partial = None
            if f > 0:
                partial = earlier_frames(layer, weights, patches[-2:])
            keep = f < frames - 1
            done = frame_step(
                layer, tiles, sections, main[f], f if layer == 0 else None,
                near_a[f], near_b[f], gains, weights, partial, keep,
            )
            if keep:
                patches.append(done[-2:])
                done = done[:-2]
            next_main.append(done if layer == sections - 1 else done[0])
            edge_a.append(done[1])
            edge_b.append(done[2])
        main = next_main

    parts = []
    for f in range(frames):
        for target in range(sections - 1):
            pairs = share_pairs(target, shape)
            parts.append(send(main[f][target], pairs))
        parts.append(main[f][sections - 1])
    return assemble(parts, frames, sections).reshape(
        frames, channels // sections, rows, width
    )


def assemble(parts, frames, sections):
    lines, width = parts[0].shape

    def kernel(*refs):
        out = refs[-1]
        for s in range(sections):

            @pl.when(lax.axis_index("section") == s)
            def _():
                for f in range(frames):
                    out[f] = refs[f * sections + s][...]

    return pl.pallas_call(
        kernel,
        out_shape=jax.ShapeDtypeStruct((frames, lines, width), jnp.float32),
        in_specs=[VMEM] * len(parts),
        out_specs=VMEM,
        compiler_params=GRANT,
        name="assemble",
    )(*parts)


def solution(mesh):
    return jax.shard_map(
        local,
        mesh=mesh,
        in_specs=(
            P("groups", None, "tiles", None),
            P("section", None, None, None),
            P("section", None),
        ),
        out_specs=P("groups", "section", "tiles", None),
        check_vma=False,
    )
```

```python
import jax
import jax.numpy as jnp
from jax import lax
from jax.experimental import pallas as pl
from jax.experimental.pallas import tpu as pltpu
from jax.sharding import PartitionSpec as P


EPSILON = 1e-06
GRANT = pltpu.CompilerParams(vmem_limit_bytes=12 * 2**20)
VMEM = pl.BlockSpec(memory_space=pltpu.VMEM)
HBM = pl.BlockSpec(memory_space=pltpu.HBM)


def partner_a(tile, tiles):
    other = tile ^ 1
    return other if other < tiles else tile


def partner_b(tile, tiles):
    other = ((tile - 1) ^ 1) + 1 if tile > 0 else tile
    return other if other < tiles else tile


def idle_cycle(where, names):
    for k, name in enumerate(names):
        where[name] = names[(k + 1) % len(names)]


def section_hop(layer, sections):
    where = {}
    if layer % 2 == 0:
        idle_cycle(where, [layer, layer + 1])
    elif layer + 2 < sections:
        idle_cycle(where, [layer - 1, layer, layer + 1, layer + 2])
    else:
        idle_cycle(where, [layer - 1, layer, layer + 1])
    taken = set(where)
    for s in range(sections):
        if s not in taken:
            where[s] = s ^ 1 if (s ^ 1) not in taken and (s ^ 1) < sections else s
    return where


def all_pairs(shape, goal):
    groups, tiles, sections = shape
    pairs = []
    for g in range(groups):
        for t in range(tiles):
            for s in range(sections):
                to_g, to_t, to_s = goal(g, t, s)
                pairs.append(
                    ((g * tiles + t) * sections + s, (to_g * tiles + to_t) * sections + to_s)
                )
    return pairs


def other_group(g, groups):
    return g ^ 1 if (g ^ 1) < groups else g


def hop_pairs(layer, shape, tile_of):
    hop = section_hop(layer, shape[2])
    return all_pairs(
        shape, lambda g, t, s: (g, tile_of(t) if s == layer else t, hop[s])
    )


def rim_pairs(shape, tile_of):
    groups, _, sections = shape

    def goal(g, t, s):
        if tile_of(t) == t and sections % 2 == 0:
            return g, t, s ^ 1
        if s == 0:
            return g, tile_of(t), s
        if s == 1 or s ^ 1 >= sections:
            return other_group(g, groups), t, s
        return g, t, s ^ 1

    return all_pairs(shape, goal)


def share_pairs(target, shape):
    groups, _, sections = shape
    last = sections - 1
    where = {}
    if target == last - 1:
        idle_cycle(where, [last, target])
    elif target == 0:
        idle_cycle(where, [last, 0, 1, last - 1])
    else:
        idle_cycle(where, [last, target, target ^ 1])

    def goal(g, t, s):
        if s in where:
            return g, t, where[s]
        if s ^ 1 not in where and s ^ 1 < sections:
            return g, t, s ^ 1
        return other_group(g, groups), t, s

    return all_pairs(shape, goal)


def send(value, pairs):
    return lax.ppermute(value, ("groups", "tiles", "section"), pairs)


def split(values):
    high = values.astype(jnp.bfloat16)
    low = (values - high.astype(jnp.float32)).astype(jnp.bfloat16)
    return high, low


def held(shape, dtype=jnp.float32):
    return pltpu.VMEM(shape, dtype)


def tap_groups(channels, depth):
    groups = []
    for k in range(0, 9, 2):
        size = min(2, 9 - k)
        extra = depth - 9 * channels if k + size == 9 else 0
        cols = slice(k * channels, (k + size) * channels + extra)
        groups.append((k, size, cols, extra))
    return groups


def fetch_taps(weight_ref, first, staged, sems, groups):
    copies = []
    for n, (k, size, _, _) in enumerate(groups):
        copies.append(
            pltpu.make_async_copy(
                weight_ref.at[pl.ds(first + k, size)],
                staged.at[pl.ds(k, size)],
                sems.at[n],
            )
        )
        copies[-1].start()
    return copies


def split_taps(copies, staged, both, groups):
    channels = staged.shape[1]
    for copy, (k, size, cols, extra) in zip(copies, groups):
        copy.wait()
        parts = [staged[k + n] for n in range(size)]
        if extra:
            parts.append(jnp.zeros((channels, extra), jnp.float32))
        upper, lower = split(jnp.concatenate(parts, axis=1))
        both[:channels, cols] = upper
        both[channels:, cols] = lower


def in_hbm(value):
    return pltpu.with_memory_space_constraint(value, pltpu.HBM)


def opening(latents, weight, gain, rows, depth):
    frames, lines, width = latents.shape
    channels = lines // rows
    groups = tap_groups(channels, depth)

    def kernel(latent_ref, weight_ref, gain_ref, *refs):
        held_ref, both, gains = refs[:3]
        outs = refs[3 : 3 + 2 * frames]
        staged, row, frame_sems, sems, gain_sem = refs[3 + 2 * frames :]
        frame_copies = []
        for f in range(frames):
            frame_copies.append(
                pltpu.make_async_copy(latent_ref.at[f], held_ref.at[f], frame_sems.at[f])
            )
            frame_copies[-1].start()
        copies = fetch_taps(weight_ref, 18, staged, sems, groups)
        gain_copy = pltpu.make_async_copy(gain_ref, row, gain_sem)
        gain_copy.start()
        even = lax.rem(lax.axis_index("tiles"), 2) == 0
        for f in range(frames):
            frame_copies[f].wait()
            top = held_ref[f, pl.ds(0, channels, stride=rows), :]
            bottom = held_ref[f, pl.ds(rows - 1, channels, stride=rows), :]
            outs[2 * f][...] = jnp.where(even, bottom, top)
            outs[2 * f + 1][...] = jnp.where(even, top, bottom)
        split_taps(copies, staged, both, groups)
        gain_copy.wait()
        square = (channels, channels)
        lane = lax.broadcasted_iota(jnp.int32, square, 1)
        sublane = lax.broadcasted_iota(jnp.int32, square, 0)
        spread = jnp.broadcast_to(row[...], square)
        column = jnp.sum(jnp.where(lane == sublane, spread, 0.0), axis=1, keepdims=True)
        gains[...] = jnp.broadcast_to(column, (channels, width))

    out_shape = [
        held(latents.shape),
        held((2 * channels, depth), jnp.bfloat16),
        held((channels, width)),
    ] + [held((channels, width))] * (2 * frames)
    return pl.pallas_call(
        kernel,
        out_shape=tuple(out_shape),
        in_specs=[HBM, HBM, HBM],
        out_specs=tuple([VMEM] * len(out_shape)),
        scratch_shapes=[
            pltpu.VMEM((9, channels, channels), jnp.float32),
            pltpu.VMEM(gain.shape, jnp.float32),
            pltpu.SemaphoreType.DMA((frames,)),
            pltpu.SemaphoreType.DMA((len(groups),)),
            pltpu.SemaphoreType.DMA,
        ],
        compiler_params=GRANT,
        name="opening",
    )(in_hbm(latents), in_hbm(weight), in_hbm(gain))


def earlier_taps(weight, offset, depth):
    channels = weight.shape[1]
    groups = tap_groups(channels, depth)

    def kernel(weight_ref, both, staged, sems):
        copies = fetch_taps(weight_ref, 9 * offset, staged, sems, groups)
        split_taps(copies, staged, both, groups)

    return pl.pallas_call(
        kernel,
        out_shape=held((2 * channels, depth), jnp.bfloat16),
        in_specs=[HBM],
        out_specs=VMEM,
        scratch_shapes=[
            pltpu.VMEM((9, channels, channels), jnp.float32),
            pltpu.SemaphoreType.DMA((len(groups),)),
        ],
        compiler_params=GRANT,
        name="earlier_taps",
    )(in_hbm(weight))


def normalize(values, gain):
    meansq = jnp.mean(values * values, axis=0, keepdims=True)
    scaled = values * lax.rsqrt(meansq + EPSILON) * gain
    return scaled / (1.0 + jnp.exp(-scaled))


def shifted(values, col_off):
    if col_off == 1:
        return values
    width = values.shape[1]
    lane = lax.broadcasted_iota(jnp.int32, values.shape, 1)
    if col_off == 0:
        return jnp.where(lane == 0, 0.0, pltpu.roll(values, 1, 1))
    return jnp.where(lane == width - 1, 0.0, pltpu.roll(values, width - 1, 1))


def product(both, patch_high, patch_low):
    def dot(a, b):
        return jnp.dot(a, b, preferred_element_type=jnp.float32)

    channels = both.shape[0] // 2
    first = dot(both, patch_high)
    return first[:channels] + first[channels:] + dot(both[:channels], patch_low)


def frame_step(layer, tiles, sections, main, frame, near_a, near_b, gain, weights, partial, keep):
    channels, width = near_a.shape[-2:]
    lines = main.shape[-2]
    rows = lines // channels
    depth = weights[-1].shape[1]
    last = layer == sections - 1
    share = lines // sections
    count = sections if last else 3

    def kernel(*refs):
        main_ref, a_ref, b_ref, gain_ref, both_ref = refs[:5]
        refs = refs[5:]
        if partial is not None:
            partial_ref, refs = refs[0], refs[1:]
        outs, (patch_high, patch_low) = refs[:count], refs[count:]
        tile = lax.axis_index("tiles")
        even = lax.rem(tile, 2) == 0

        @pl.when(lax.axis_index("section") == layer)
        def _():
            gains = gain_ref[...]
            near_one, near_two = a_ref[...], b_ref[...]
            above = jnp.where(even, near_two, near_one)
            below = jnp.where(even, near_one, near_two)
            above = jnp.where(tile == 0, 0.0, above)
            below = jnp.where(tile == tiles - 1, 0.0, below)
            own = []
            for r in range(rows):
                line = pl.ds(r, channels, stride=rows)
                own.append(main_ref[line, :] if frame is None else main_ref[frame, line, :])
            if depth > 9 * channels:
                pad = jnp.zeros((depth - 9 * channels, rows * width), jnp.bfloat16)
                patch_high[9 * channels :, :] = pad
                patch_low[9 * channels :, :] = pad
            for q, source in enumerate([above] + own + [below]):
                normed = normalize(source, gains)
                for e in range(3):
                    upper, lower = split(shifted(normed, e))
                    for b in range(3):
                        r = q - b
                        if 0 <= r < rows:
                            k = (3 * b + e) * channels
                            cols = slice(r * width, (r + 1) * width)
                            patch_high[k : k + channels, cols] = upper
                            patch_low[k : k + channels, cols] = lower
            total = product(both_ref[...], patch_high[...], patch_low[...])
            if partial is not None:
                total = total + partial_ref[...]
            results = [
                own[r] + total[:, r * width : (r + 1) * width] for r in range(rows)
            ]
            if last:
                part = share // rows
                for s in range(sections):
                    for r in range(rows):
                        outs[s][pl.ds(r, part, stride=rows), :] = results[r][
                            s * part : (s + 1) * part
                        ]
            else:
                for r in range(rows):
                    outs[0][pl.ds(r, channels, stride=rows), :] = results[r]
                outs[1][...] = jnp.where(even, results[-1], results[0])
                outs[2][...] = jnp.where(even, results[0], results[-1])

    operands = [main, near_a, near_b, gain, weights[-1]]
    if partial is not None:
        operands.append(partial)
    if last:
        out_shape = [held((share, width))] * sections
    else:
        edge = held((channels, width))
        out_shape = [held((lines, width)), edge, edge]
    patch = held((depth, rows * width), jnp.bfloat16)
    scratch = []
    if keep:
        out_shape += [patch, patch]
    else:
        scratch = [patch, patch]
    return pl.pallas_call(
        kernel,
        out_shape=tuple(out_shape),
        in_specs=[VMEM] * len(operands),
        out_specs=tuple([VMEM] * len(out_shape)),
        scratch_shapes=scratch,
        cost_estimate=pl.CostEstimate(
            flops=6 * channels * depth * rows * width,
            bytes_accessed=2**20,
            transcendentals=0,
        ),
        compiler_params=GRANT,
        name="frame_step",
    )(*operands)


def earlier_frames(layer, weights, patches):
    channels, depth = weights[-1].shape[0] // 2, weights[-1].shape[1]
    count = len(patches)
    columns = patches[0][0].shape[1]

    taps = weights[len(weights) - 1 - count : len(weights) - 1]

    def kernel(*refs):
        out_ref = refs[-1]

        @pl.when(lax.axis_index("section") == layer)
        def _():
            total = None
            for n in range(count):
                high, low = refs[count + 2 * n], refs[count + 2 * n + 1]
                term = product(refs[n][...], high[...], low[...])
                total = term if total is None else total + term
            out_ref[...] = total

    operands = [*taps]
    for pair in patches:
        operands += list(pair)
    return pl.pallas_call(
        kernel,
        out_shape=held((channels, columns)),
        in_specs=[VMEM] * len(operands),
        out_specs=VMEM,
        cost_estimate=pl.CostEstimate(
            flops=6 * channels * depth * columns * count,
            bytes_accessed=2**20,
            transcendentals=0,
        ),
        compiler_params=GRANT,
        name="earlier_frames",
    )(*operands)


def local(latents, conv_weight, gain):
    frames, channels, rows, width = latents.shape
    tiles, sections = lax.axis_size("tiles"), lax.axis_size("section")
    shape = (lax.axis_size("groups"), tiles, sections)
    depth = -(-9 * channels // 256) * 256
    steps = min(frames, 3)
    of_a = lambda t: partner_a(t, tiles)
    of_b = lambda t: partner_b(t, tiles)

    flat = latents.reshape(frames, channels * rows, width)
    flat, current, gains, *edge = opening(flat, conv_weight[0], gain, rows, depth)
    edge_a, edge_b = edge[0::2], edge[1::2]
    rim_a, rim_b = (rim_pairs(shape, of) for of in (of_a, of_b))
    near_a = [send(edge_a[f], rim_a) for f in range(frames)]
    near_b = [send(edge_b[f], rim_b) for f in range(frames)]
    earlier = [earlier_taps(conv_weight[0], a, depth) for a in range(3 - steps, 2)]
    weights = [*earlier, current]
    main = [flat] * frames

    for layer in range(sections):
        if layer > 0:
            straight = hop_pairs(layer - 1, shape, lambda t: t)
            cross_a = hop_pairs(layer - 1, shape, of_a)
            cross_b = hop_pairs(layer - 1, shape, of_b)
            main = [send(main[f], straight) for f in range(frames)]
            near_a = [send(edge_a[f], cross_a) for f in range(frames)]
            near_b = [send(edge_b[f], cross_b) for f in range(frames)]
        patches, next_main, edge_a, edge_b = [], [], [], []
        for f in range(frames):
            partial = None
            if f > 0:
                partial = earlier_frames(layer, weights, patches[-2:])
            keep = f < frames - 1
            done = frame_step(
                layer, tiles, sections, main[f], f if layer == 0 else None,
                near_a[f], near_b[f], gains, weights, partial, keep,
            )
            if keep:
                patches.append(done[-2:])
                done = done[:-2]
            next_main.append(done if layer == sections - 1 else done[0])
            edge_a.append(done[1])
            edge_b.append(done[2])
        main = next_main

    parts = []
    for f in range(frames):
        for target in range(sections - 1):
            pairs = share_pairs(target, shape)
            parts.append(send(main[f][target], pairs))
        parts.append(main[f][sections - 1])
    return assemble(parts, frames, sections).reshape(
        frames, channels // sections, rows, width
    )


def assemble(parts, frames, sections):
    lines, width = parts[0].shape

    def kernel(*refs):
        out = refs[-1]
        for s in range(sections):

            @pl.when(lax.axis_index("section") == s)
            def _():
                for f in range(frames):
                    out[f] = refs[f * sections + s][...]

    return pl.pallas_call(
        kernel,
        out_shape=jax.ShapeDtypeStruct((frames, lines, width), jnp.float32),
        in_specs=[VMEM] * len(parts),
        out_specs=VMEM,
        compiler_params=GRANT,
        name="assemble",
    )(*parts)


def solution(mesh):
    return jax.shard_map(
        local,
        mesh=mesh,
        in_specs=(
            P("groups", None, "tiles", None),
            P("section", None, None, None),
            P("section", None),
        ),
        out_specs=P("groups", "section", "tiles", None),
        check_vma=False,
    )
```

```python
import jax
import jax.numpy as jnp
from jax import lax
from jax.experimental import pallas as pl
from jax.experimental.pallas import tpu as pltpu
from jax.sharding import PartitionSpec as P


EPSILON = 1e-06
GRANT = pltpu.CompilerParams(vmem_limit_bytes=12 * 2**20)
VMEM = pl.BlockSpec(memory_space=pltpu.VMEM)
HBM = pl.BlockSpec(memory_space=pltpu.HBM)


def partner_a(tile, tiles):
    other = tile ^ 1
    return other if other < tiles else tile


def partner_b(tile, tiles):
    other = ((tile - 1) ^ 1) + 1 if tile > 0 else tile
    return other if other < tiles else tile


def idle_cycle(where, names):
    for k, name in enumerate(names):
        where[name] = names[(k + 1) % len(names)]


def section_hop(layer, sections):
    where = {}
    if layer % 2 == 0:
        idle_cycle(where, [layer, layer + 1])
    elif layer + 2 < sections:
        idle_cycle(where, [layer - 1, layer, layer + 1, layer + 2])
    else:
        idle_cycle(where, [layer - 1, layer, layer + 1])
    taken = set(where)
    for s in range(sections):
        if s not in taken:
            where[s] = s ^ 1 if (s ^ 1) not in taken and (s ^ 1) < sections else s
    return where


def all_pairs(shape, goal):
    groups, tiles, sections = shape
    pairs = []
    for g in range(groups):
        for t in range(tiles):
            for s in range(sections):
                to_g, to_t, to_s = goal(g, t, s)
                pairs.append(
                    ((g * tiles + t) * sections + s, (to_g * tiles + to_t) * sections + to_s)
                )
    return pairs


def other_group(g, groups):
    return g ^ 1 if (g ^ 1) < groups else g


def hop_pairs(layer, shape, tile_of):
    hop = section_hop(layer, shape[2])
    return all_pairs(
        shape, lambda g, t, s: (g, tile_of(t) if s == layer else t, hop[s])
    )


def rim_pairs(shape, tile_of):
    groups, _, sections = shape

    def goal(g, t, s):
        if tile_of(t) == t and sections % 2 == 0:
            return g, t, s ^ 1
        if s == 0:
            return g, tile_of(t), s
        if s == 1 or s ^ 1 >= sections:
            return other_group(g, groups), t, s
        return g, t, s ^ 1

    return all_pairs(shape, goal)


def share_pairs(target, shape):
    groups, _, sections = shape
    last = sections - 1
    where = {}
    if target == last - 1:
        idle_cycle(where, [last, target])
    elif target == 0:
        idle_cycle(where, [last, 0, 1, last - 1])
    else:
        idle_cycle(where, [last, target, target ^ 1])

    def goal(g, t, s):
        if s in where:
            return g, t, where[s]
        if s ^ 1 not in where and s ^ 1 < sections:
            return g, t, s ^ 1
        return other_group(g, groups), t, s

    return all_pairs(shape, goal)


def send(value, pairs):
    return lax.ppermute(value, ("groups", "tiles", "section"), pairs)


def split(values):
    high = values.astype(jnp.bfloat16)
    low = (values - high.astype(jnp.float32)).astype(jnp.bfloat16)
    return high, low


def held(shape, dtype=jnp.float32):
    return pltpu.VMEM(shape, dtype)


def prepare(weight, steps, depth):
    channels = weight.shape[1]

    def kernel(weight_ref, *outs):
        for both, a in zip(outs, range(3 - steps, 3)):
            for k in range(0, 9, 2):
                size = min(2, 9 - k)
                parts = [weight_ref[9 * a + k + n] for n in range(size)]
                cols = slice(k * channels, (k + size) * channels)
                if k + size == 9 and depth > 9 * channels:
                    extra = depth - 9 * channels
                    parts.append(jnp.zeros((channels, extra), jnp.float32))
                    cols = slice(k * channels, depth)
                upper, lower = split(jnp.concatenate(parts, axis=1))
                both[:channels, cols] = upper
                both[channels:, cols] = lower

    out_shape = [held((2 * channels, depth), jnp.bfloat16)] * steps
    return pl.pallas_call(
        kernel,
        out_shape=tuple(out_shape),
        in_specs=[VMEM],
        out_specs=tuple([VMEM] * steps),
        compiler_params=GRANT,
        name="prepare",
    )(weight)


def in_hbm(value):
    return pltpu.with_memory_space_constraint(value, pltpu.HBM)


def opening(latents, gain, rows):
    frames, lines, width = latents.shape
    channels = lines // rows

    def kernel(latent_ref, gain_ref, *refs):
        held_ref, gains = refs[:2]
        outs = refs[2 : 2 + 2 * frames]
        row, frame_sems, gain_sem = refs[2 + 2 * frames :]
        gain_copy = pltpu.make_async_copy(gain_ref, row, gain_sem)
        gain_copy.start()
        frame_copies = []
        for f in range(frames):
            frame_copies.append(
                pltpu.make_async_copy(latent_ref.at[f], held_ref.at[f], frame_sems.at[f])
            )
            frame_copies[-1].start()
        gain_copy.wait()
        square = (channels, channels)
        lane = lax.broadcasted_iota(jnp.int32, square, 1)
        sublane = lax.broadcasted_iota(jnp.int32, square, 0)
        spread = jnp.broadcast_to(row[...], square)
        column = jnp.sum(jnp.where(lane == sublane, spread, 0.0), axis=1, keepdims=True)
        gains[...] = jnp.broadcast_to(column, (channels, width))
        even = lax.rem(lax.axis_index("tiles"), 2) == 0
        for f in range(frames):
            frame_copies[f].wait()
            top = held_ref[f, pl.ds(0, channels, stride=rows), :]
            bottom = held_ref[f, pl.ds(rows - 1, channels, stride=rows), :]
            outs[2 * f][...] = jnp.where(even, bottom, top)
            outs[2 * f + 1][...] = jnp.where(even, top, bottom)

    out_shape = [held(latents.shape), held((channels, width))]
    out_shape += [held((channels, width))] * (2 * frames)
    return pl.pallas_call(
        kernel,
        out_shape=tuple(out_shape),
        in_specs=[HBM, HBM],
        out_specs=tuple([VMEM] * len(out_shape)),
        scratch_shapes=[
            pltpu.VMEM(gain.shape, jnp.float32),
            pltpu.SemaphoreType.DMA((frames,)),
            pltpu.SemaphoreType.DMA,
        ],
        compiler_params=GRANT,
        cost_estimate=pl.CostEstimate(
            flops=2 * 10**9, bytes_accessed=2**20, transcendentals=0
        ),
        name="opening",
    )(in_hbm(latents), in_hbm(gain))


def normalize(values, gain):
    meansq = jnp.mean(values * values, axis=0, keepdims=True)
    scaled = values * lax.rsqrt(meansq + EPSILON) * gain
    return scaled / (1.0 + jnp.exp(-scaled))


def shifted(values, col_off):
    if col_off == 1:
        return values
    width = values.shape[1]
    lane = lax.broadcasted_iota(jnp.int32, values.shape, 1)
    if col_off == 0:
        return jnp.where(lane == 0, 0.0, pltpu.roll(values, 1, 1))
    return jnp.where(lane == width - 1, 0.0, pltpu.roll(values, width - 1, 1))


def product(both, patch_high, patch_low):
    def dot(a, b):
        return jnp.dot(a, b, preferred_element_type=jnp.float32)

    channels = both.shape[0] // 2
    first = dot(both, patch_high)
    return first[:channels] + first[channels:] + dot(both[:channels], patch_low)


def frame_step(layer, tiles, sections, main, frame, near_a, near_b, gain, weights, partial, keep):
    channels, width = near_a.shape[-2:]
    lines = main.shape[-2]
    rows = lines // channels
    depth = weights[-1].shape[1]
    last = layer == sections - 1
    share = lines // sections
    count = sections if last else 3

    def kernel(*refs):
        main_ref, a_ref, b_ref, gain_ref, both_ref = refs[:5]
        refs = refs[5:]
        if partial is not None:
            partial_ref, refs = refs[0], refs[1:]
        outs, (patch_high, patch_low) = refs[:count], refs[count:]
        tile = lax.axis_index("tiles")
        even = lax.rem(tile, 2) == 0

        @pl.when(lax.axis_index("section") == layer)
        def _():
            gains = gain_ref[...]
            near_one, near_two = a_ref[...], b_ref[...]
            above = jnp.where(even, near_two, near_one)
            below = jnp.where(even, near_one, near_two)
            above = jnp.where(tile == 0, 0.0, above)
            below = jnp.where(tile == tiles - 1, 0.0, below)
            own = []
            for r in range(rows):
                line = pl.ds(r, channels, stride=rows)
                own.append(main_ref[line, :] if frame is None else main_ref[frame, line, :])
            if depth > 9 * channels:
                pad = jnp.zeros((depth - 9 * channels, rows * width), jnp.bfloat16)
                patch_high[9 * channels :, :] = pad
                patch_low[9 * channels :, :] = pad
            for q, source in enumerate([above] + own + [below]):
                normed = normalize(source, gains)
                for e in range(3):
                    upper, lower = split(shifted(normed, e))
                    for b in range(3):
                        r = q - b
                        if 0 <= r < rows:
                            k = (3 * b + e) * channels
                            cols = slice(r * width, (r + 1) * width)
                            patch_high[k : k + channels, cols] = upper
                            patch_low[k : k + channels, cols] = lower
            total = product(both_ref[...], patch_high[...], patch_low[...])
            if partial is not None:
                total = total + partial_ref[...]
            results = [
                own[r] + total[:, r * width : (r + 1) * width] for r in range(rows)
            ]
            if last:
                part = share // rows
                for s in range(sections):
                    for r in range(rows):
                        outs[s][pl.ds(r, part, stride=rows), :] = results[r][
                            s * part : (s + 1) * part
                        ]
            else:
                for r in range(rows):
                    outs[0][pl.ds(r, channels, stride=rows), :] = results[r]
                outs[1][...] = jnp.where(even, results[-1], results[0])
                outs[2][...] = jnp.where(even, results[0], results[-1])

    operands = [main, near_a, near_b, gain, weights[-1]]
    if partial is not None:
        operands.append(partial)
    if last:
        out_shape = [held((share, width))] * sections
    else:
        edge = held((channels, width))
        out_shape = [held((lines, width)), edge, edge]
    patch = held((depth, rows * width), jnp.bfloat16)
    scratch = []
    if keep:
        out_shape += [patch, patch]
    else:
        scratch = [patch, patch]
    return pl.pallas_call(
        kernel,
        out_shape=tuple(out_shape),
        in_specs=[VMEM] * len(operands),
        out_specs=tuple([VMEM] * len(out_shape)),
        scratch_shapes=scratch,
        cost_estimate=pl.CostEstimate(
            flops=6 * channels * depth * rows * width,
            bytes_accessed=2**20,
            transcendentals=0,
        ),
        compiler_params=GRANT,
        name="frame_step",
    )(*operands)


def earlier_frames(layer, weights, patches):
    channels, depth = weights[-1].shape[0] // 2, weights[-1].shape[1]
    count = len(patches)
    columns = patches[0][0].shape[1]

    taps = weights[len(weights) - 1 - count : len(weights) - 1]

    def kernel(*refs):
        out_ref = refs[-1]

        @pl.when(lax.axis_index("section") == layer)
        def _():
            total = None
            for n in range(count):
                high, low = refs[count + 2 * n], refs[count + 2 * n + 1]
                term = product(refs[n][...], high[...], low[...])
                total = term if total is None else total + term
            out_ref[...] = total

    operands = [*taps]
    for pair in patches:
        operands += list(pair)
    return pl.pallas_call(
        kernel,
        out_shape=held((channels, columns)),
        in_specs=[VMEM] * len(operands),
        out_specs=VMEM,
        cost_estimate=pl.CostEstimate(
            flops=6 * channels * depth * columns * count,
            bytes_accessed=2**20,
            transcendentals=0,
        ),
        compiler_params=GRANT,
        name="earlier_frames",
    )(*operands)


def local(latents, conv_weight, gain):
    frames, channels, rows, width = latents.shape
    tiles, sections = lax.axis_size("tiles"), lax.axis_size("section")
    shape = (lax.axis_size("groups"), tiles, sections)
    depth = -(-9 * channels // 256) * 256
    steps = min(frames, 3)
    of_a = lambda t: partner_a(t, tiles)
    of_b = lambda t: partner_b(t, tiles)

    flat = latents.reshape(frames, channels * rows, width)
    flat, gains, *edge = opening(flat, gain, rows)
    edge_a, edge_b = edge[0::2], edge[1::2]
    rim_a, rim_b = (rim_pairs(shape, of) for of in (of_a, of_b))
    near_a = [send(edge_a[f], rim_a) for f in range(frames)]
    near_b = [send(edge_b[f], rim_b) for f in range(frames)]
    weights = prepare(conv_weight[0], steps, depth)
    main = [flat] * frames

    for layer in range(sections):
        if layer > 0:
            straight = hop_pairs(layer - 1, shape, lambda t: t)
            cross_a = hop_pairs(layer - 1, shape, of_a)
            cross_b = hop_pairs(layer - 1, shape, of_b)
            main = [send(main[f], straight) for f in range(frames)]
            near_a = [send(edge_a[f], cross_a) for f in range(frames)]
            near_b = [send(edge_b[f], cross_b) for f in range(frames)]
        patches, next_main, edge_a, edge_b = [], [], [], []
        for f in range(frames):
            partial = None
            if f > 0:
                partial = earlier_frames(layer, weights, patches[-2:])
            keep = f < frames - 1
            done = frame_step(
                layer, tiles, sections, main[f], f if layer == 0 else None,
                near_a[f], near_b[f], gains, weights, partial, keep,
            )
            if keep:
                patches.append(done[-2:])
                done = done[:-2]
            next_main.append(done if layer == sections - 1 else done[0])
            edge_a.append(done[1])
            edge_b.append(done[2])
        main = next_main

    parts = []
    for f in range(frames):
        for target in range(sections - 1):
            pairs = share_pairs(target, shape)
            parts.append(send(main[f][target], pairs))
        parts.append(main[f][sections - 1])
    return assemble(parts, frames, sections).reshape(
        frames, channels // sections, rows, width
    )


def assemble(parts, frames, sections):
    lines, width = parts[0].shape

    def kernel(*refs):
        out = refs[-1]
        for s in range(sections):

            @pl.when(lax.axis_index("section") == s)
            def _():
                for f in range(frames):
                    out[f] = refs[f * sections + s][...]

    return pl.pallas_call(
        kernel,
        out_shape=jax.ShapeDtypeStruct((frames, lines, width), jnp.float32),
        in_specs=[VMEM] * len(parts),
        out_specs=VMEM,
        compiler_params=GRANT,
        name="assemble",
    )(*parts)


def solution(mesh):
    return jax.shard_map(
        local,
        mesh=mesh,
        in_specs=(
            P("groups", None, "tiles", None),
            P("section", None, None, None),
            P("section", None),
        ),
        out_specs=P("groups", "section", "tiles", None),
        check_vma=False,
    )
```

```python
import jax
import jax.numpy as jnp
from jax import lax
from jax.experimental import pallas as pl
from jax.experimental.pallas import tpu as pltpu
from jax.sharding import PartitionSpec as P


EPSILON = 1e-06
GRANT = pltpu.CompilerParams(vmem_limit_bytes=12 * 2**20)
VMEM = pl.BlockSpec(memory_space=pltpu.VMEM)
HBM = pl.BlockSpec(memory_space=pltpu.HBM)


def partner_a(tile, tiles):
    other = tile ^ 1
    return other if other < tiles else tile


def partner_b(tile, tiles):
    other = ((tile - 1) ^ 1) + 1 if tile > 0 else tile
    return other if other < tiles else tile


def idle_cycle(where, names):
    for k, name in enumerate(names):
        where[name] = names[(k + 1) % len(names)]


def section_hop(layer, sections, early=False):
    where = {}
    if early and layer + 3 < sections:
        idle_cycle(where, [layer, layer + 1, layer + 2, layer + 3])
    elif layer % 2 == 0:
        idle_cycle(where, [layer, layer + 1])
    elif layer + 2 < sections:
        idle_cycle(where, [layer - 1, layer, layer + 1, layer + 2])
    else:
        idle_cycle(where, [layer - 1, layer, layer + 1])
    taken = set(where)
    for s in range(sections):
        if s not in taken:
            where[s] = s ^ 1 if (s ^ 1) not in taken and (s ^ 1) < sections else s
    return where


def all_pairs(shape, goal):
    groups, tiles, sections = shape
    pairs = []
    for g in range(groups):
        for t in range(tiles):
            for s in range(sections):
                to_g, to_t, to_s = goal(g, t, s)
                pairs.append(
                    ((g * tiles + t) * sections + s, (to_g * tiles + to_t) * sections + to_s)
                )
    return pairs


def other_group(g, groups):
    return g ^ 1 if (g ^ 1) < groups else g


def hop_pairs(layer, shape, tile_of, early=False):
    hop = section_hop(layer, shape[2], early)
    return all_pairs(
        shape, lambda g, t, s: (g, tile_of(t) if s == layer else t, hop[s])
    )


def rim_pairs(shape, tile_of):
    groups, _, sections = shape

    def goal(g, t, s):
        if tile_of(t) == t and sections % 2 == 0:
            return g, t, s ^ 1
        if s == 0:
            return g, tile_of(t), s
        if s == 1 or s ^ 1 >= sections:
            return other_group(g, groups), t, s
        return g, t, s ^ 1

    return all_pairs(shape, goal)


def share_pairs(target, shape):
    groups, _, sections = shape
    last = sections - 1
    where = {}
    if target == last - 1:
        idle_cycle(where, [last, target])
    elif target == 0:
        idle_cycle(where, [last, 0, 1, last - 1])
    else:
        idle_cycle(where, [last, target, target ^ 1])

    def goal(g, t, s):
        if s in where:
            return g, t, where[s]
        if s ^ 1 not in where and s ^ 1 < sections:
            return g, t, s ^ 1
        return other_group(g, groups), t, s

    return all_pairs(shape, goal)


def send(value, pairs):
    return lax.ppermute(value, ("groups", "tiles", "section"), pairs)


def split(values):
    high = values.astype(jnp.bfloat16)
    low = (values - high.astype(jnp.float32)).astype(jnp.bfloat16)
    return high, low


def held(shape, dtype=jnp.float32):
    return pltpu.VMEM(shape, dtype)


def prepare(weight, steps, depth):
    channels = weight.shape[1]

    def kernel(weight_ref, *outs):
        for both, a in zip(outs, range(3 - steps, 3)):
            for k in range(0, 9, 2):
                size = min(2, 9 - k)
                parts = [weight_ref[9 * a + k + n] for n in range(size)]
                cols = slice(k * channels, (k + size) * channels)
                if k + size == 9 and depth > 9 * channels:
                    extra = depth - 9 * channels
                    parts.append(jnp.zeros((channels, extra), jnp.float32))
                    cols = slice(k * channels, depth)
                upper, lower = split(jnp.concatenate(parts, axis=1))
                both[:channels, cols] = upper
                both[channels:, cols] = lower

    out_shape = [held((2 * channels, depth), jnp.bfloat16)] * steps
    return pl.pallas_call(
        kernel,
        out_shape=tuple(out_shape),
        in_specs=[VMEM],
        out_specs=tuple([VMEM] * steps),
        compiler_params=GRANT,
        name="prepare",
    )(weight)


def in_hbm(value):
    return pltpu.with_memory_space_constraint(value, pltpu.HBM)


def opening(latents, gain, rows):
    frames, lines, width = latents.shape
    channels = lines // rows

    def kernel(latent_ref, gain_ref, *refs):
        held_ref, gains = refs[:2]
        outs = refs[2 : 2 + 2 * frames]
        row, frame_sems, gain_sem = refs[2 + 2 * frames :]
        gain_copy = pltpu.make_async_copy(gain_ref, row, gain_sem)
        gain_copy.start()
        frame_copies = []
        for f in range(frames):
            frame_copies.append(
                pltpu.make_async_copy(latent_ref.at[f], held_ref.at[f], frame_sems.at[f])
            )
            frame_copies[-1].start()
        gain_copy.wait()
        square = (channels, channels)
        lane = lax.broadcasted_iota(jnp.int32, square, 1)
        sublane = lax.broadcasted_iota(jnp.int32, square, 0)
        spread = jnp.broadcast_to(row[...], square)
        column = jnp.sum(jnp.where(lane == sublane, spread, 0.0), axis=1, keepdims=True)
        gains[...] = jnp.broadcast_to(column, (channels, width))
        even = lax.rem(lax.axis_index("tiles"), 2) == 0
        for f in range(frames):
            frame_copies[f].wait()
            top = held_ref[f, pl.ds(0, channels, stride=rows), :]
            bottom = held_ref[f, pl.ds(rows - 1, channels, stride=rows), :]
            outs[2 * f][...] = jnp.where(even, bottom, top)
            outs[2 * f + 1][...] = jnp.where(even, top, bottom)

    out_shape = [held(latents.shape), held((channels, width))]
    out_shape += [held((channels, width))] * (2 * frames)
    return pl.pallas_call(
        kernel,
        out_shape=tuple(out_shape),
        in_specs=[HBM, HBM],
        out_specs=tuple([VMEM] * len(out_shape)),
        scratch_shapes=[
            pltpu.VMEM(gain.shape, jnp.float32),
            pltpu.SemaphoreType.DMA((frames,)),
            pltpu.SemaphoreType.DMA,
        ],
        compiler_params=GRANT,
        cost_estimate=pl.CostEstimate(
            flops=2 * 10**9, bytes_accessed=2**20, transcendentals=0
        ),
        name="opening",
    )(in_hbm(latents), in_hbm(gain))


def normalize(values, gain):
    meansq = jnp.mean(values * values, axis=0, keepdims=True)
    scaled = values * lax.rsqrt(meansq + EPSILON) * gain
    return scaled / (1.0 + jnp.exp(-scaled))


def shifted(values, col_off):
    if col_off == 1:
        return values
    width = values.shape[1]
    lane = lax.broadcasted_iota(jnp.int32, values.shape, 1)
    if col_off == 0:
        return jnp.where(lane == 0, 0.0, pltpu.roll(values, 1, 1))
    return jnp.where(lane == width - 1, 0.0, pltpu.roll(values, width - 1, 1))


def product(both, patch_high, patch_low):
    def dot(a, b):
        return jnp.dot(a, b, preferred_element_type=jnp.float32)

    channels = both.shape[0] // 2
    first = dot(both, patch_high)
    return first[:channels] + first[channels:] + dot(both[:channels], patch_low)


def frame_step(layer, tiles, sections, main, frame, near_a, near_b, gain, weights, partial, keep):
    channels, width = near_a.shape[-2:]
    lines = main.shape[-2]
    rows = lines // channels
    depth = weights[-1].shape[1]
    last = layer == sections - 1
    share = lines // sections
    count = sections if last else 3

    def kernel(*refs):
        main_ref, a_ref, b_ref, gain_ref, both_ref = refs[:5]
        refs = refs[5:]
        if partial is not None:
            partial_ref, refs = refs[0], refs[1:]
        outs, (patch_high, patch_low) = refs[:count], refs[count:]
        tile = lax.axis_index("tiles")
        even = lax.rem(tile, 2) == 0

        @pl.when(lax.axis_index("section") == layer)
        def _():
            gains = gain_ref[...]
            near_one, near_two = a_ref[...], b_ref[...]
            above = jnp.where(even, near_two, near_one)
            below = jnp.where(even, near_one, near_two)
            above = jnp.where(tile == 0, 0.0, above)
            below = jnp.where(tile == tiles - 1, 0.0, below)
            own = []
            for r in range(rows):
                line = pl.ds(r, channels, stride=rows)
                own.append(main_ref[line, :] if frame is None else main_ref[frame, line, :])
            if depth > 9 * channels:
                pad = jnp.zeros((depth - 9 * channels, rows * width), jnp.bfloat16)
                patch_high[9 * channels :, :] = pad
                patch_low[9 * channels :, :] = pad
            for q, source in enumerate([above] + own + [below]):
                normed = normalize(source, gains)
                for e in range(3):
                    upper, lower = split(shifted(normed, e))
                    for b in range(3):
                        r = q - b
                        if 0 <= r < rows:
                            k = (3 * b + e) * channels
                            cols = slice(r * width, (r + 1) * width)
                            patch_high[k : k + channels, cols] = upper
                            patch_low[k : k + channels, cols] = lower
            total = product(both_ref[...], patch_high[...], patch_low[...])
            if partial is not None:
                total = total + partial_ref[...]
            results = [
                own[r] + total[:, r * width : (r + 1) * width] for r in range(rows)
            ]
            if last:
                part = share // rows
                for s in range(sections):
                    for r in range(rows):
                        outs[s][pl.ds(r, part, stride=rows), :] = results[r][
                            s * part : (s + 1) * part
                        ]
            else:
                for r in range(rows):
                    outs[0][pl.ds(r, channels, stride=rows), :] = results[r]
                outs[1][...] = jnp.where(even, results[-1], results[0])
                outs[2][...] = jnp.where(even, results[0], results[-1])

    operands = [main, near_a, near_b, gain, weights[-1]]
    if partial is not None:
        operands.append(partial)
    if last:
        out_shape = [held((share, width))] * sections
    else:
        edge = held((channels, width))
        out_shape = [held((lines, width)), edge, edge]
    patch = held((depth, rows * width), jnp.bfloat16)
    scratch = []
    if keep:
        out_shape += [patch, patch]
    else:
        scratch = [patch, patch]
    return pl.pallas_call(
        kernel,
        out_shape=tuple(out_shape),
        in_specs=[VMEM] * len(operands),
        out_specs=tuple([VMEM] * len(out_shape)),
        scratch_shapes=scratch,
        cost_estimate=pl.CostEstimate(
            flops=6 * channels * depth * rows * width,
            bytes_accessed=2**20,
            transcendentals=0,
        ),
        compiler_params=GRANT,
        name="frame_step",
    )(*operands)


def earlier_frames(layer, weights, patches):
    channels, depth = weights[-1].shape[0] // 2, weights[-1].shape[1]
    count = len(patches)
    columns = patches[0][0].shape[1]

    taps = weights[len(weights) - 1 - count : len(weights) - 1]

    def kernel(*refs):
        out_ref = refs[-1]

        @pl.when(lax.axis_index("section") == layer)
        def _():
            total = None
            for n in range(count):
                high, low = refs[count + 2 * n], refs[count + 2 * n + 1]
                term = product(refs[n][...], high[...], low[...])
                total = term if total is None else total + term
            out_ref[...] = total

    operands = [*taps]
    for pair in patches:
        operands += list(pair)
    return pl.pallas_call(
        kernel,
        out_shape=held((channels, columns)),
        in_specs=[VMEM] * len(operands),
        out_specs=VMEM,
        cost_estimate=pl.CostEstimate(
            flops=6 * channels * depth * columns * count,
            bytes_accessed=2**20,
            transcendentals=0,
        ),
        compiler_params=GRANT,
        name="earlier_frames",
    )(*operands)


def local(latents, conv_weight, gain):
    frames, channels, rows, width = latents.shape
    tiles, sections = lax.axis_size("tiles"), lax.axis_size("section")
    shape = (lax.axis_size("groups"), tiles, sections)
    depth = -(-9 * channels // 256) * 256
    steps = min(frames, 3)
    of_a = lambda t: partner_a(t, tiles)
    of_b = lambda t: partner_b(t, tiles)

    flat = latents.reshape(frames, channels * rows, width)
    flat, gains, *edge = opening(flat, gain, rows)
    edge_a, edge_b = edge[0::2], edge[1::2]
    rim_a, rim_b = (rim_pairs(shape, of) for of in (of_a, of_b))
    near_a = [send(edge_a[f], rim_a) for f in range(frames)]
    near_b = [send(edge_b[f], rim_b) for f in range(frames)]
    weights = prepare(conv_weight[0], steps, depth)
    main = [flat] * frames

    for layer in range(sections):
        if layer > 0:
            early = layer == 1
            straight = hop_pairs(layer - 1, shape, lambda t: t)
            cross_a = hop_pairs(layer - 1, shape, of_a, early)
            cross_b = hop_pairs(layer - 1, shape, of_b)
            main = [send(main[f], straight) for f in range(frames)]
            near_a = [send(edge_a[f], cross_a) for f in range(frames)]
            near_b = [send(edge_b[f], cross_b) for f in range(frames)]
        patches, next_main, edge_a, edge_b = [], [], [], []
        for f in range(frames):
            partial = None
            if f > 0:
                partial = earlier_frames(layer, weights, patches[-2:])
            keep = f < frames - 1
            done = frame_step(
                layer, tiles, sections, main[f], f if layer == 0 else None,
                near_a[f], near_b[f], gains, weights, partial, keep,
            )
            if keep:
                patches.append(done[-2:])
                done = done[:-2]
            next_main.append(done if layer == sections - 1 else done[0])
            edge_a.append(done[1])
            edge_b.append(done[2])
        main = next_main

    parts = []
    for f in range(frames):
        for target in range(sections - 1):
            pairs = share_pairs(target, shape)
            parts.append(send(main[f][target], pairs))
        parts.append(main[f][sections - 1])
    return assemble(parts, frames, sections).reshape(
        frames, channels // sections, rows, width
    )


def assemble(parts, frames, sections):
    lines, width = parts[0].shape

    def kernel(*refs):
        out = refs[-1]
        for s in range(sections):

            @pl.when(lax.axis_index("section") == s)
            def _():
                for f in range(frames):
                    out[f] = refs[f * sections + s][...]

    return pl.pallas_call(
        kernel,
        out_shape=jax.ShapeDtypeStruct((frames, lines, width), jnp.float32),
        in_specs=[VMEM] * len(parts),
        out_specs=VMEM,
        compiler_params=GRANT,
        name="assemble",
    )(*parts)


def solution(mesh):
    return jax.shard_map(
        local,
        mesh=mesh,
        in_specs=(
            P("groups", None, "tiles", None),
            P("section", None, None, None),
            P("section", None),
        ),
        out_specs=P("groups", "section", "tiles", None),
        check_vma=False,
    )
```

```python
import jax
import jax.numpy as jnp
from jax import lax
from jax.experimental import pallas as pl
from jax.experimental.pallas import tpu as pltpu
from jax.sharding import PartitionSpec as P


EPSILON = 1e-06
GRANT = pltpu.CompilerParams(vmem_limit_bytes=12 * 2**20)
VMEM = pl.BlockSpec(memory_space=pltpu.VMEM)
HBM = pl.BlockSpec(memory_space=pltpu.HBM)


def partner_a(tile, tiles):
    other = tile ^ 1
    return other if other < tiles else tile


def partner_b(tile, tiles):
    other = ((tile - 1) ^ 1) + 1 if tile > 0 else tile
    return other if other < tiles else tile


def idle_cycle(where, names):
    for k, name in enumerate(names):
        where[name] = names[(k + 1) % len(names)]


def section_hop(layer, sections, early=False):
    where = {}
    spare = layer + 2 if layer == 0 else layer - 2
    if early and spare + 1 < sections:
        idle_cycle(where, [layer, layer + 1, spare, spare + 1])
    elif layer % 2 == 0:
        idle_cycle(where, [layer, layer + 1])
    elif layer + 2 < sections:
        idle_cycle(where, [layer - 1, layer, layer + 1, layer + 2])
    else:
        idle_cycle(where, [layer - 1, layer, layer + 1])
    taken = set(where)
    for s in range(sections):
        if s not in taken:
            where[s] = s ^ 1 if (s ^ 1) not in taken and (s ^ 1) < sections else s
    return where


def all_pairs(shape, goal):
    groups, tiles, sections = shape
    pairs = []
    for g in range(groups):
        for t in range(tiles):
            for s in range(sections):
                to_g, to_t, to_s = goal(g, t, s)
                pairs.append(
                    ((g * tiles + t) * sections + s, (to_g * tiles + to_t) * sections + to_s)
                )
    return pairs


def other_group(g, groups):
    return g ^ 1 if (g ^ 1) < groups else g


def hop_pairs(layer, shape, tile_of, early=False):
    hop = section_hop(layer, shape[2], early)
    return all_pairs(
        shape, lambda g, t, s: (g, tile_of(t) if s == layer else t, hop[s])
    )


def rim_pairs(shape, tile_of):
    groups, _, sections = shape

    def goal(g, t, s):
        if tile_of(t) == t and sections % 2 == 0:
            return g, t, s ^ 1
        if s == 0:
            return g, tile_of(t), s
        if s == 1 or s ^ 1 >= sections:
            return other_group(g, groups), t, s
        return g, t, s ^ 1

    return all_pairs(shape, goal)


def share_pairs(target, shape):
    groups, _, sections = shape
    last = sections - 1
    where = {}
    if target == last - 1:
        idle_cycle(where, [last, target])
    elif target == 0:
        idle_cycle(where, [last, 0, last - 1])
    else:
        idle_cycle(where, [last, target, target ^ 1])

    def goal(g, t, s):
        if s in where:
            return g, t, where[s]
        if s ^ 1 not in where and s ^ 1 < sections:
            return g, t, s ^ 1
        return other_group(g, groups), t, s

    return all_pairs(shape, goal)


def send(value, pairs):
    return lax.ppermute(value, ("groups", "tiles", "section"), pairs)


def split(values):
    high = values.astype(jnp.bfloat16)
    low = (values - high.astype(jnp.float32)).astype(jnp.bfloat16)
    return high, low


def held(shape, dtype=jnp.float32):
    return pltpu.VMEM(shape, dtype)


def prepare(weight, steps, depth):
    channels = weight.shape[1]

    def kernel(weight_ref, *outs):
        for both, a in zip(outs, range(3 - steps, 3)):
            for k in range(0, 9, 2):
                size = min(2, 9 - k)
                parts = [weight_ref[9 * a + k + n] for n in range(size)]
                cols = slice(k * channels, (k + size) * channels)
                if k + size == 9 and depth > 9 * channels:
                    extra = depth - 9 * channels
                    parts.append(jnp.zeros((channels, extra), jnp.float32))
                    cols = slice(k * channels, depth)
                upper, lower = split(jnp.concatenate(parts, axis=1))
                both[:channels, cols] = upper
                both[channels:, cols] = lower

    out_shape = [held((2 * channels, depth), jnp.bfloat16)] * steps
    return pl.pallas_call(
        kernel,
        out_shape=tuple(out_shape),
        in_specs=[VMEM],
        out_specs=tuple([VMEM] * steps),
        compiler_params=GRANT,
        name="prepare",
    )(weight)


def in_hbm(value):
    return pltpu.with_memory_space_constraint(value, pltpu.HBM)


def opening(latents, gain, rows):
    frames, lines, width = latents.shape
    channels = lines // rows

    def kernel(latent_ref, gain_ref, *refs):
        held_ref, gains = refs[:2]
        outs = refs[2 : 2 + 2 * frames]
        row, frame_sems, gain_sem = refs[2 + 2 * frames :]
        gain_copy = pltpu.make_async_copy(gain_ref, row, gain_sem)
        gain_copy.start()
        frame_copies = []
        for f in range(frames):
            frame_copies.append(
                pltpu.make_async_copy(latent_ref.at[f], held_ref.at[f], frame_sems.at[f])
            )
            frame_copies[-1].start()
        gain_copy.wait()
        square = (channels, channels)
        lane = lax.broadcasted_iota(jnp.int32, square, 1)
        sublane = lax.broadcasted_iota(jnp.int32, square, 0)
        spread = jnp.broadcast_to(row[...], square)
        column = jnp.sum(jnp.where(lane == sublane, spread, 0.0), axis=1, keepdims=True)
        gains[...] = jnp.broadcast_to(column, (channels, width))
        even = lax.rem(lax.axis_index("tiles"), 2) == 0
        for f in range(frames):
            frame_copies[f].wait()
            top = held_ref[f, pl.ds(0, channels, stride=rows), :]
            bottom = held_ref[f, pl.ds(rows - 1, channels, stride=rows), :]
            outs[2 * f][...] = jnp.where(even, bottom, top)
            outs[2 * f + 1][...] = jnp.where(even, top, bottom)

    out_shape = [held(latents.shape), held((channels, width))]
    out_shape += [held((channels, width))] * (2 * frames)
    return pl.pallas_call(
        kernel,
        out_shape=tuple(out_shape),
        in_specs=[HBM, HBM],
        out_specs=tuple([VMEM] * len(out_shape)),
        scratch_shapes=[
            pltpu.VMEM(gain.shape, jnp.float32),
            pltpu.SemaphoreType.DMA((frames,)),
            pltpu.SemaphoreType.DMA,
        ],
        compiler_params=GRANT,
        cost_estimate=pl.CostEstimate(
            flops=2 * 10**9, bytes_accessed=2**20, transcendentals=0
        ),
        name="opening",
    )(in_hbm(latents), in_hbm(gain))


def normalize(values, gain):
    meansq = jnp.mean(values * values, axis=0, keepdims=True)
    scaled = values * lax.rsqrt(meansq + EPSILON) * gain
    return scaled / (1.0 + jnp.exp(-scaled))


def shifted(values, col_off):
    if col_off == 1:
        return values
    width = values.shape[1]
    lane = lax.broadcasted_iota(jnp.int32, values.shape, 1)
    if col_off == 0:
        return jnp.where(lane == 0, 0.0, pltpu.roll(values, 1, 1))
    return jnp.where(lane == width - 1, 0.0, pltpu.roll(values, width - 1, 1))


def product(both, patch_high, patch_low):
    def dot(a, b):
        return jnp.dot(a, b, preferred_element_type=jnp.float32)

    channels = both.shape[0] // 2
    first = dot(both, patch_high)
    return first[:channels] + first[channels:] + dot(both[:channels], patch_low)


def frame_step(layer, tiles, sections, main, frame, near_a, near_b, gain, weights, partial, keep):
    channels, width = near_a.shape[-2:]
    lines = main.shape[-2]
    rows = lines // channels
    depth = weights[-1].shape[1]
    last = layer == sections - 1
    share = lines // sections
    count = sections if last else 3

    def kernel(*refs):
        main_ref, a_ref, b_ref, gain_ref, both_ref = refs[:5]
        refs = refs[5:]
        if partial is not None:
            partial_ref, refs = refs[0], refs[1:]
        outs, (patch_high, patch_low) = refs[:count], refs[count:]
        tile = lax.axis_index("tiles")
        even = lax.rem(tile, 2) == 0

        @pl.when(lax.axis_index("section") == layer)
        def _():
            gains = gain_ref[...]
            near_one, near_two = a_ref[...], b_ref[...]
            above = jnp.where(even, near_two, near_one)
            below = jnp.where(even, near_one, near_two)
            above = jnp.where(tile == 0, 0.0, above)
            below = jnp.where(tile == tiles - 1, 0.0, below)
            own = []
            for r in range(rows):
                line = pl.ds(r, channels, stride=rows)
                own.append(main_ref[line, :] if frame is None else main_ref[frame, line, :])
            if depth > 9 * channels:
                pad = jnp.zeros((depth - 9 * channels, rows * width), jnp.bfloat16)
                patch_high[9 * channels :, :] = pad
                patch_low[9 * channels :, :] = pad
            for q, source in enumerate([above] + own + [below]):
                normed = normalize(source, gains)
                for e in range(3):
                    upper, lower = split(shifted(normed, e))
                    for b in range(3):
                        r = q - b
                        if 0 <= r < rows:
                            k = (3 * b + e) * channels
                            cols = slice(r * width, (r + 1) * width)
                            patch_high[k : k + channels, cols] = upper
                            patch_low[k : k + channels, cols] = lower
            total = product(both_ref[...], patch_high[...], patch_low[...])
            if partial is not None:
                total = total + partial_ref[...]
            results = [
                own[r] + total[:, r * width : (r + 1) * width] for r in range(rows)
            ]
            if last:
                part = share // rows
                for s in range(sections):
                    for r in range(rows):
                        outs[s][pl.ds(r, part, stride=rows), :] = results[r][
                            s * part : (s + 1) * part
                        ]
            else:
                for r in range(rows):
                    outs[0][pl.ds(r, channels, stride=rows), :] = results[r]
                outs[1][...] = jnp.where(even, results[-1], results[0])
                outs[2][...] = jnp.where(even, results[0], results[-1])

    operands = [main, near_a, near_b, gain, weights[-1]]
    if partial is not None:
        operands.append(partial)
    if last:
        out_shape = [held((share, width))] * sections
    else:
        edge = held((channels, width))
        out_shape = [held((lines, width)), edge, edge]
    patch = held((depth, rows * width), jnp.bfloat16)
    scratch = []
    if keep:
        out_shape += [patch, patch]
    else:
        scratch = [patch, patch]
    return pl.pallas_call(
        kernel,
        out_shape=tuple(out_shape),
        in_specs=[VMEM] * len(operands),
        out_specs=tuple([VMEM] * len(out_shape)),
        scratch_shapes=scratch,
        cost_estimate=pl.CostEstimate(
            flops=6 * channels * depth * rows * width,
            bytes_accessed=2**20,
            transcendentals=0,
        ),
        compiler_params=GRANT,
        name="frame_step",
    )(*operands)


def earlier_frames(layer, weights, patches):
    channels, depth = weights[-1].shape[0] // 2, weights[-1].shape[1]
    count = len(patches)
    columns = patches[0][0].shape[1]

    taps = weights[len(weights) - 1 - count : len(weights) - 1]

    def kernel(*refs):
        out_ref = refs[-1]

        @pl.when(lax.axis_index("section") == layer)
        def _():
            total = None
            for n in range(count):
                high, low = refs[count + 2 * n], refs[count + 2 * n + 1]
                term = product(refs[n][...], high[...], low[...])
                total = term if total is None else total + term
            out_ref[...] = total

    operands = [*taps]
    for pair in patches:
        operands += list(pair)
    return pl.pallas_call(
        kernel,
        out_shape=held((channels, columns)),
        in_specs=[VMEM] * len(operands),
        out_specs=VMEM,
        cost_estimate=pl.CostEstimate(
            flops=6 * channels * depth * columns * count,
            bytes_accessed=2**20,
            transcendentals=0,
        ),
        compiler_params=GRANT,
        name="earlier_frames",
    )(*operands)


def local(latents, conv_weight, gain):
    frames, channels, rows, width = latents.shape
    tiles, sections = lax.axis_size("tiles"), lax.axis_size("section")
    shape = (lax.axis_size("groups"), tiles, sections)
    depth = -(-9 * channels // 256) * 256
    steps = min(frames, 3)
    of_a = lambda t: partner_a(t, tiles)
    of_b = lambda t: partner_b(t, tiles)

    flat = latents.reshape(frames, channels * rows, width)
    flat, gains, *edge = opening(flat, gain, rows)
    edge_a, edge_b = edge[0::2], edge[1::2]
    rim_a, rim_b = (rim_pairs(shape, of) for of in (of_a, of_b))
    near_a = [send(edge_a[f], rim_a) for f in range(frames)]
    near_b = [send(edge_b[f], rim_b) for f in range(frames)]
    weights = prepare(conv_weight[0], steps, depth)
    main = [flat] * frames

    for layer in range(sections):
        if layer > 0:
            straight = hop_pairs(layer - 1, shape, lambda t: t)
            cross_a = [
                hop_pairs(layer - 1, shape, of_a, layer == 1 or (layer % 2 == 1 and f > 0))
                for f in range(frames)
            ]
            cross_b = hop_pairs(layer - 1, shape, of_b)
            main = [send(main[f], straight) for f in range(frames)]
            near_a = [send(edge_a[f], cross_a[f]) for f in range(frames)]
            near_b = [send(edge_b[f], cross_b) for f in range(frames)]
        patches, next_main, edge_a, edge_b = [], [], [], []
        for f in range(frames):
            partial = None
            if f > 0:
                partial = earlier_frames(layer, weights, patches[-2:])
            keep = f < frames - 1
            done = frame_step(
                layer, tiles, sections, main[f], f if layer == 0 else None,
                near_a[f], near_b[f], gains, weights, partial, keep,
            )
            if keep:
                patches.append(done[-2:])
                done = done[:-2]
            next_main.append(done if layer == sections - 1 else done[0])
            edge_a.append(done[1])
            edge_b.append(done[2])
        main = next_main

    parts = []
    for f in range(frames):
        for target in range(sections - 1):
            pairs = share_pairs(target, shape)
            parts.append(send(main[f][target], pairs))
        parts.append(main[f][sections - 1])
    return assemble(parts, frames, sections).reshape(
        frames, channels // sections, rows, width
    )


def assemble(parts, frames, sections):
    lines, width = parts[0].shape

    def kernel(*refs):
        out = refs[-1]
        for s in range(sections):

            @pl.when(lax.axis_index("section") == s)
            def _():
                for f in range(frames):
                    out[f] = refs[f * sections + s][...]

    return pl.pallas_call(
        kernel,
        out_shape=jax.ShapeDtypeStruct((frames, lines, width), jnp.float32),
        in_specs=[VMEM] * len(parts),
        out_specs=VMEM,
        compiler_params=GRANT,
        name="assemble",
    )(*parts)


def solution(mesh):
    return jax.shard_map(
        local,
        mesh=mesh,
        in_specs=(
            P("groups", None, "tiles", None),
            P("section", None, None, None),
            P("section", None),
        ),
        out_specs=P("groups", "section", "tiles", None),
        check_vma=False,
    )
```
